512 devices in a mesh: roll: 64 (over y_hi, z, x), seq: 8 (over y_lo, core).
Axes of the slice: x: 4, y: 8 (y_hi: 2, y_lo: 4; y = y_hi * 4 + y_lo), z: 8, core: 2. Of those that a mesh axis runs over, the one named last changes fastest.
Arguments:
- hidden: bfloat16 [64, 4096, 2880], P('roll', 'seq'), may hold values from -6 to 6
- key_value_blocks: bfloat16 [2880, 1024], P('roll'), may hold values from -0.109375 to 0.109375
- block_of: int32 [64], replicated, may hold values from 0 to 63, each once
- queries: bfloat16 [64, 256, 4096], P('roll', 'seq'), may hold values from -480 to 480
- key_pos: int32 [64, 4096], P('roll', 'seq'), may hold values from 0 to 8190, as said below
- query_pos: int32 [64, 256], P('roll', 'seq'), may hold values from 0 to 8190, as said below
Outputs:
- context: bfloat16 [64, 256, 4096], P('roll', 'seq')
The draws below stay inside these ranges and needn't reach their ends.
Inputs may be any that keep to these rules, and one draw needn't show every extreme that they name: Along each sequence key_pos rises by one from that sequence's start; starts lie in 0 to 4095 and some sequence starts at 0, another at 4095. `query_pos`: each query position lies between the first and the last key position of its sequence.
All inputs are finite; a program needn't handle non-finite values.
Results may differ from the reference program's by a relative error of at most 0.017.
The reference program's roundings to bfloat16 on the way count: a program that leaves them out, or rounds other values in their place, can miss the bound.
Values may be sent and summed in bfloat16 or wider, within the bound.
No kernel may reach another device: no remote copies, remote signals or barrier semaphores. Data moves between devices by JAX's collectives and lax.ppermute only.
A program may use at most 64 MiB of HBM per device.

```python
import jax
import jax.numpy as jnp
from jax import lax

MODEL_WIDTH = 2880
QUERY_HEAD_COUNT = 64
KEY_VALUE_HEADS = 8
HEAD_WIDTH = 64
CACHED_LENGTH = 4096
QUERY_ROW_COUNT = 256
N_ROLL = 64


def position_helper(key):
    folded = jax.random.fold_in(key, 7)
    key_one, key_two, key_three, key_four = jax.random.split(folded, 4)
    starts = jax.random.randint(key_one, (N_ROLL,), 0, 4096)
    chosen = jax.random.randint(key_three, (), 0, N_ROLL)
    starts = starts.at[chosen].set(4095)
    starts = starts.at[(chosen + 1) % N_ROLL].set(0)
    offsets = jax.random.randint(key_two, (N_ROLL, QUERY_ROW_COUNT), 0, CACHED_LENGTH)
    column = jax.random.randint(key_four, (), 0, QUERY_ROW_COUNT)
    offsets = offsets.at[chosen, column].set(CACHED_LENGTH - 1)
    key_positions = starts[:, None] + jnp.arange(CACHED_LENGTH)[None, :]
    query_positions = starts[:, None] + offsets
    return (key_positions.astype(jnp.int32), query_positions.astype(jnp.int32))


def draw_key_pos(key, part):
    return position_helper(key)[0]


def draw_query_pos(key, part):
    return position_helper(key)[1]


def draw_queries(key, part):
    folded = jax.random.fold_in(key, 11)
    key_one = jax.random.fold_in(folded, 0)
    values = jnp.clip(jax.random.normal(key_one, (N_ROLL, QUERY_ROW_COUNT, QUERY_HEAD_COUNT * HEAD_WIDTH), jnp.float32), -6.0, 6.0)
    return values.astype(jnp.bfloat16)


def block_levels(stream_key, shape, cuts, low, high):
    gain = 1.0
    for dim, shards_of in cuts:
        steps = jax.random.uniform(jax.random.fold_in(jax.random.fold_in(stream_key, 6), dim), (shards_of,), jnp.float32, low / len(cuts), high / len(cuts))
        gain = gain * jnp.repeat(jnp.exp(steps), shape[dim] // shards_of).reshape((-1,) + (1,) * (len(shape) - 1 - dim))
    return gain


def scatter_about(stream_key, dims, spread, most, cuts=(), kind=jnp.bfloat16):
    loudness = block_levels(stream_key, dims, cuts, -0.22, 0.18) if cuts else 1.0
    entries = jax.random.normal(stream_key, dims, jnp.float32) * spread * loudness
    return jnp.minimum(jnp.maximum(entries, -most), most).astype(kind)


def setup_inputs(seed: int = 0) -> dict:
    splits = jax.random.split(jax.random.key(seed), 7)
    hidden = scatter_about(splits[0], (N_ROLL, CACHED_LENGTH, MODEL_WIDTH), 1.0, 6.0, ((0, 64), (1, 8)))
    key_value_blocks = scatter_about(splits[1], (MODEL_WIDTH, 2 * KEY_VALUE_HEADS * HEAD_WIDTH), MODEL_WIDTH ** -0.5, 0.109375, ((0, 64),))
    block_of = jax.random.permutation(splits[2], N_ROLL).astype(jnp.int32)
    queries = draw_queries(jax.random.fold_in(splits[6], 71), 0)
    key_pos = draw_key_pos(jax.random.fold_in(splits[6], 71), 0)
    query_pos = draw_query_pos(jax.random.fold_in(splits[6], 71), 0)
    return dict(hidden=hidden, key_value_blocks=key_value_blocks, block_of=block_of, queries=queries, key_pos=key_pos, query_pos=query_pos)


rope_base = 150000.0

def rotary(vectors, positions):
    head_size = vectors.shape[-1]
    half = head_size // 2
    freq = rope_base ** (-(jnp.arange(half).astype(jnp.float32) * 2.0 / head_size))
    angle = positions.astype(jnp.float32)[:, None] * freq[None, :]
    cosine = jnp.cos(angle)[:, None, :]
    sine = jnp.sin(angle)[:, None, :]
    first = vectors[..., :half]
    second = vectors[..., half:]
    return jnp.concatenate([first * cosine - second * sine, second * cosine + first * sine], axis=-1)

def reference(hidden, key_value_blocks, block_of, queries, key_pos, query_pos):
    block_rows = MODEL_WIDTH // N_ROLL
    column_slice = 2 * KEY_VALUE_HEADS * HEAD_WIDTH
    query_group = QUERY_HEAD_COUNT // KEY_VALUE_HEADS
    stored = key_value_blocks.reshape(N_ROLL, block_rows, column_slice)
    kv_weight = jnp.zeros_like(stored).at[block_of].set(stored).reshape(MODEL_WIDTH, column_slice)

    def one_sequence(index):
        projected_rows = jnp.dot(hidden[index], kv_weight, preferred_element_type=jnp.float32)
        projected_rows = projected_rows.reshape(CACHED_LENGTH, KEY_VALUE_HEADS, 2 * HEAD_WIDTH)
        keys = rotary(projected_rows[..., :HEAD_WIDTH], key_pos[index]).astype(jnp.bfloat16)
        values = projected_rows[..., HEAD_WIDTH:].astype(jnp.bfloat16)
        rotated_rows = rotary(queries[index].astype(jnp.float32).reshape(QUERY_ROW_COUNT, QUERY_HEAD_COUNT, HEAD_WIDTH), query_pos[index])
        rotated_rows = rotated_rows.astype(jnp.bfloat16).reshape(QUERY_ROW_COUNT, KEY_VALUE_HEADS, query_group, HEAD_WIDTH)
        row_pos = jnp.repeat(query_pos[index], query_group)

        def single_head(head):
            query_rows = lax.dynamic_index_in_dim(rotated_rows, head, 1, False).reshape(QUERY_ROW_COUNT * query_group, HEAD_WIDTH)
            head_keys = lax.dynamic_index_in_dim(keys, head, 1, False)
            head_values = lax.dynamic_index_in_dim(values, head, 1, False)
            scores = jnp.dot(query_rows, head_keys.T, preferred_element_type=jnp.float32) * (1.0 / jnp.sqrt(jnp.float32(HEAD_WIDTH)))
            allowed = key_pos[index][None, :] <= row_pos[:, None]
            scores = jnp.where(allowed, scores, -1e+30)
            top = lax.optimization_barrier(jnp.max(scores, axis=1, keepdims=True))
            expo = jnp.where(allowed, jnp.exp(scores - top), 0.0)
            probs = (expo / lax.optimization_barrier(jnp.sum(expo, axis=1, keepdims=True))).astype(jnp.bfloat16)
            return jnp.dot(probs, head_values, preferred_element_type=jnp.float32).astype(jnp.bfloat16)
        head_outputs = lax.map(single_head, jnp.arange(KEY_VALUE_HEADS))
        head_outputs = head_outputs.reshape(KEY_VALUE_HEADS, QUERY_ROW_COUNT, query_group * HEAD_WIDTH).transpose(1, 0, 2)
        return head_outputs.reshape(QUERY_ROW_COUNT, QUERY_HEAD_COUNT * HEAD_WIDTH)
    return lax.map(one_sequence, jnp.arange(N_ROLL))
```

```python
import functools

import jax
import jax.numpy as jnp
import numpy as np
from jax import lax
from jax.experimental import pallas as pl
from jax.experimental.pallas import tpu as pltpu
from jax.sharding import Mesh, PartitionSpec as P

HEADS = 64
KV_HEADS = 8
WIDTH = 64
GROUP = HEADS // KV_HEADS
LANES = 2 * WIDTH
ROPE_BASE = 150000.0
PAD_ROWS = 48
QUERY_BLOCK = 32
KEY_BLOCK = 512
ROLL = ("yh", "z", "x")
SEQ = ("yl", "co")


def lane_frequencies(lanes):
    half = WIDTH // 2
    freq = ROPE_BASE ** (-(jnp.arange(half).astype(jnp.float32) * 2.0 / WIDTH))
    return jnp.tile(freq, lanes // half)


def ring(size, step):
    return [(i, (i + step) % size) for i in range(size)]


def reorder_kernel(source_ref, hidden_ref, out_ref):
    depth = hidden_ref.shape[1]
    index = lax.broadcasted_iota(jnp.int32, (depth, source_ref.shape[1]), 0)
    pick = jnp.where(index == source_ref[...], 1.0, 0.0).astype(jnp.bfloat16)
    out_ref[...] = jnp.dot(
        hidden_ref[...], pick, preferred_element_type=jnp.float32
    ).astype(jnp.bfloat16)


def reorder(hidden, source):
    rows, depth = hidden.shape
    columns = source.shape[1]
    tile = 256
    return pl.pallas_call(
        reorder_kernel,
        grid=(columns // tile,),
        in_specs=[
            pl.BlockSpec((1, tile), lambda i: (0, i)),
            pl.BlockSpec((rows, depth), lambda i: (0, 0)),
        ],
        out_specs=pl.BlockSpec((rows, tile), lambda i: (0, i)),
        out_shape=jax.ShapeDtypeStruct((rows, columns), jnp.bfloat16),
        name="reorder_hidden",
    )(source, hidden)


def swap_halves(x, lane):
    half = WIDTH // 2
    return jnp.where(
        lane % WIDTH < half,
        pltpu.roll(x, LANES - half, 1),
        pltpu.roll(x, half, 1),
    )


def project_kernel(core_ref, own_ref, other_ref, *rest):
    pieces, (cos_ref, sin_ref, out_ref) = rest[:-3], rest[-3:]
    rows = own_ref.shape[0]
    core = core_ref[0]
    lane = lax.broadcasted_iota(jnp.int32, (rows, LANES), 1)
    for hidden_ref, place in ((own_ref, core), (other_ref, 1 - core)):
        total = None
        offset = 0
        for piece in pieces:
            size = piece.shape[0]
            part = jnp.dot(
                hidden_ref[:, offset : offset + size],
                piece[...],
                preferred_element_type=jnp.float32,
            )
            total = part if total is None else total + part
            offset += size
        base = pl.multiple_of(place * rows, rows)
        cosine = cos_ref[pl.ds(base, rows), :]
        sine = sin_ref[pl.ds(base, rows), :]
        for head in range(out_ref.shape[0]):
            x = total[:, head * LANES : (head + 1) * LANES]
            out_ref[head, pl.ds(base, rows), :] = (
                x * cosine + swap_halves(x, lane) * sine
            ).astype(jnp.bfloat16)


def project(core, own, other, pieces, cosine, sine):
    rows = own.shape[0]
    heads = pieces[0].shape[1] // LANES
    vmem = pl.BlockSpec(memory_space=pltpu.VMEM)
    return pl.pallas_call(
        project_kernel,
        in_specs=[pl.BlockSpec(memory_space=pltpu.SMEM)] + [vmem] * (len(pieces) + 4),
        out_specs=vmem,
        out_shape=jax.ShapeDtypeStruct((heads, 2 * rows, LANES), jnp.bfloat16),
        name="project",
    )(core, own, other, *pieces, cosine, sine)


def prepare_kernel(query_ref, pick_ref, cos_ref, sin_ref, out_ref):
    rows = query_ref.shape[0]
    lane = lax.broadcasted_iota(jnp.int32, (rows, LANES), 1)
    pick = pick_ref[...]
    for pair in range(GROUP // 2):
        x = jnp.dot(
            pick,
            query_ref[:, pair * LANES : (pair + 1) * LANES],
            preferred_element_type=jnp.float32,
        )
        x = x * cos_ref[...] + swap_halves(x, lane) * sin_ref[...]
        x = x.astype(jnp.bfloat16).astype(jnp.float32) * (1.0 / 8.0)
        first = jnp.where(lane < WIDTH, x, 0.0).astype(jnp.bfloat16)
        second = jnp.where(lane < WIDTH, pltpu.roll(x, WIDTH, 1), 0.0).astype(jnp.bfloat16)
        for block in range(rows // QUERY_BLOCK):
            here = slice(block * QUERY_BLOCK, (block + 1) * QUERY_BLOCK)
            for head, value in ((2 * pair, first), (2 * pair + 1, second)):
                out_ref[block, head * QUERY_BLOCK : (head + 1) * QUERY_BLOCK, :] = value[here]


def prepare(query, pick, cosine, sine):
    rows = query.shape[0]
    vmem = pl.BlockSpec(memory_space=pltpu.VMEM)
    return pl.pallas_call(
        prepare_kernel,
        in_specs=[vmem] * 4,
        out_specs=vmem,
        out_shape=jax.ShapeDtypeStruct(
            (rows // QUERY_BLOCK, GROUP * QUERY_BLOCK, LANES), jnp.bfloat16
        ),
        name="prepare_queries",
    )(query, pick, cosine, sine)


def attend_kernel(
    bound_ref, query_ref, kv_ref, last_ref, unpick_ref, out_ref, value_ref, sorted_ref
):
    blocks = query_ref.shape[0]
    rows = query_ref.shape[1]
    keys = kv_ref.shape[0]
    lane_kv = lax.broadcasted_iota(jnp.int32, (KEY_BLOCK, LANES), 1)
    for step in range(keys // KEY_BLOCK):
        here = slice(step * KEY_BLOCK, (step + 1) * KEY_BLOCK)
        value_ref[here, :] = jnp.where(
            lane_kv < WIDTH, jnp.ones((), jnp.bfloat16), kv_ref[here, :]
        )
    column = lax.broadcasted_iota(jnp.int32, (rows, KEY_BLOCK), 1)
    lane = lax.broadcasted_iota(jnp.int32, (QUERY_BLOCK, LANES), 1)

    def one_block(block, carry):
        query = query_ref[block]
        last = last_ref[block]

        def step(masked, index, state):
            top, total = state
            base = pl.multiple_of(index * KEY_BLOCK, KEY_BLOCK)
            scores = lax.dot_general(
                query,
                kv_ref[pl.ds(base, KEY_BLOCK), :],
                (((1,), (1,)), ((), ())),
                preferred_element_type=jnp.float32,
            )
            if masked:
                scores = jnp.where(column <= last - base, scores, -1e30)
            new_top = jnp.maximum(top, jnp.max(scores, axis=1, keepdims=True))
            expo = jnp.exp(scores - new_top)
            part = jnp.dot(
                expo.astype(jnp.bfloat16),
                value_ref[pl.ds(base, KEY_BLOCK), :],
                preferred_element_type=jnp.float32,
            )
            return new_top, total * jnp.exp(top - new_top) + part

        state = (
            jnp.full((rows, 1), -1e30, jnp.float32),
            jnp.zeros((rows, LANES), jnp.float32),
        )
        full = bound_ref[0, block]
        state = lax.fori_loop(0, full, functools.partial(step, False), state)
        _, total = lax.fori_loop(full, bound_ref[1, block], functools.partial(step, True), state)
        result = total / pltpu.roll(total, WIDTH, 1)
        place = pl.multiple_of(block * QUERY_BLOCK, QUERY_BLOCK)
        for pair in range(GROUP // 2):
            even = result[2 * pair * QUERY_BLOCK : (2 * pair + 1) * QUERY_BLOCK]
            odd = result[(2 * pair + 1) * QUERY_BLOCK : (2 * pair + 2) * QUERY_BLOCK]
            sorted_ref[pl.ds(place, QUERY_BLOCK), pair * LANES : (pair + 1) * LANES] = jnp.where(
                lane < WIDTH, pltpu.roll(even, WIDTH, 1), odd
            ).astype(jnp.bfloat16)
        return carry

    lax.fori_loop(0, blocks, one_block, 0)
    out_ref[...] = jnp.dot(
        unpick_ref[...], sorted_ref[...], preferred_element_type=jnp.float32
    ).astype(jnp.bfloat16)


def attend(bounds, query, kv, last, unpick):
    vmem = pl.BlockSpec(memory_space=pltpu.VMEM)
    count = unpick.shape[0]
    return pl.pallas_call(
        attend_kernel,
        in_specs=[pl.BlockSpec(memory_space=pltpu.SMEM)] + [vmem] * 4,
        out_specs=vmem,
        out_shape=jax.ShapeDtypeStruct((count, GROUP * WIDTH), jnp.bfloat16),
        scratch_shapes=[
            pltpu.VMEM(kv.shape, jnp.bfloat16),
            pltpu.VMEM((count, GROUP * WIDTH), jnp.bfloat16),
        ],
        name="attend",
    )(bounds, query, kv, last, unpick)


def gather_weight(blocks):
    block_rows = blocks.shape[0]
    core = lax.axis_index("co")
    split = blocks.reshape(block_rows, KV_HEADS // 2, 2, LANES)
    mine = lax.dynamic_index_in_dim(split, core, 2, False).reshape(block_rows, -1)
    mine = jnp.pad(mine, ((0, PAD_ROWS - block_rows), (0, 0)))
    far = lax.ppermute(mine, "yh", ring(2, 1))
    both = jnp.concatenate([mine, far], 0)
    plane = lax.all_to_all(
        jnp.broadcast_to(both[None], (8,) + both.shape), "z", 0, 0, tiled=True
    )
    plane = plane.reshape(8 * 2 * PAD_ROWS, -1)
    half = plane.shape[0] // 2
    below = lax.ppermute(plane, "x", ring(4, 1))
    above = lax.ppermute(plane, "x", ring(4, -1))
    across_low = lax.ppermute(below[:half], "x", ring(4, 1))
    across_high = lax.ppermute(above[half:], "x", ring(4, -1))
    return plane, below, above, across_low, across_high


def slot_order(block_of):
    yh, z, x = (lax.axis_index(a) for a in ROLL)
    xs = jnp.stack([x, x + 3, x + 1, x + 2]) % 4
    ys = jnp.stack([yh, 1 - yh])
    stored = (
        ys[None, None, :] * 32 + jnp.arange(8)[None, :, None] * 4 + xs[:, None, None]
    ).reshape(-1)
    return block_of[stored]


def shards(hidden, blocks, block_of, queries, key_pos, query_pos):
    core = lax.axis_index("co")
    seq_index = lax.axis_index(SEQ)
    seq = lax.axis_size(SEQ)
    rows = hidden.shape[1]
    keys = rows * seq
    block_rows = blocks.shape[0]
    query_rows = queries.shape[1]
    start = key_pos[0, 0] - rows * seq_index

    slots = slot_order(block_of)
    inner = jnp.arange(PAD_ROWS)
    source = jnp.where(
        inner[None, :] < block_rows, slots[:, None] * block_rows + inner[None, :], -1
    ).reshape(1, -1)

    high = (query_pos[0] >> 8).astype(jnp.bfloat16)
    low = (query_pos[0] & 255).astype(jnp.bfloat16)
    extra = jnp.concatenate(
        [
            jnp.broadcast_to(high[:, None, None], (query_rows, KV_HEADS, WIDTH)),
            jnp.broadcast_to(low[:, None, None], (query_rows, KV_HEADS, WIDTH)),
        ],
        -1,
    )
    payload = jnp.concatenate([queries[0].reshape(query_rows, KV_HEADS, GROUP * WIDTH), extra], -1)
    payload = lax.all_to_all(payload.transpose(1, 0, 2), SEQ, 0, 0, tiled=True)

    pieces = gather_weight(blocks)
    own = reorder(hidden[0], source)
    other = lax.ppermute(own, "co", ring(2, 1))

    total_queries = query_rows * seq
    payload = payload.reshape(total_queries, -1)
    query = payload[:, : GROUP * WIDTH]
    positions = (
        payload[:, GROUP * WIDTH].astype(jnp.float32) * 256.0
        + payload[:, GROUP * WIDTH + WIDTH].astype(jnp.float32)
    ).astype(jnp.int32)
    order = jnp.arange(total_queries)
    before = (positions[None, :] < positions[:, None]) | (
        (positions[None, :] == positions[:, None]) & (order[None, :] < order[:, None])
    )
    rank = jnp.sum(before.astype(jnp.int32), axis=1)
    pick_mask = rank[None, :] == order[:, None]
    sorted_pos = jnp.sum(jnp.where(pick_mask, positions[None, :], 0), axis=1)
    pick = pick_mask.astype(jnp.bfloat16)
    unpick = (rank[:, None] == order[None, :]).astype(jnp.bfloat16)
    last = sorted_pos - start
    by_block = last.reshape(-1, QUERY_BLOCK)
    bounds = jnp.stack(
        [(by_block[:, 0] + 1) // KEY_BLOCK, by_block[:, -1] // KEY_BLOCK + 1]
    )
    last_rows = jnp.tile(by_block, (1, GROUP))[..., None]

    sign = jnp.asarray(np.where(np.arange(LANES) % WIDTH < WIDTH // 2, -1.0, 1.0), jnp.float32)
    freq = lane_frequencies(LANES)
    query_angle = sorted_pos.astype(jnp.float32)[:, None] * freq[None, :]
    prepared = prepare(query, pick, jnp.cos(query_angle), jnp.sin(query_angle) * sign)

    is_key = jnp.arange(LANES) < WIDTH
    chip_rows = 2 * rows
    chip_pos = start + chip_rows * lax.axis_index("yl") + jnp.arange(chip_rows)
    key_angle = chip_pos.astype(jnp.float32)[:, None] * jnp.where(is_key, freq, 0.0)[None, :]
    key_sine = jnp.sin(key_angle) * jnp.where(is_key, sign, 0.0)

    kv = project(core.reshape(1), own, other, pieces, jnp.cos(key_angle), key_sine)
    kv = lax.all_to_all(kv, "yl", 0, 0, tiled=True).reshape(keys, LANES)
    context = attend(bounds, prepared, kv, last_rows, unpick)
    context = context.reshape(seq, query_rows, GROUP * WIDTH)
    context = lax.all_to_all(context, SEQ, 0, 0, tiled=True)
    return context.transpose(1, 0, 2).reshape(1, query_rows, HEADS * WIDTH)


def solution(mesh):
    fine = Mesh(mesh.devices.reshape(2, 8, 4, 4, 2), ROLL + SEQ)
    return jax.shard_map(
        shards,
        mesh=fine,
        in_specs=(
            P(ROLL, SEQ, None),
            P(ROLL, None),
            P(),
            P(ROLL, SEQ, None),
            P(ROLL, SEQ),
            P(ROLL, SEQ),
        ),
        out_specs=P(ROLL, SEQ, None),
        check_vma=False,
    )
```

```python
import functools

import jax
import jax.numpy as jnp
import numpy as np
from jax import lax
from jax.experimental import pallas as pl
from jax.experimental.pallas import tpu as pltpu
from jax.sharding import Mesh, PartitionSpec as P


HEADS = 64
KV_HEADS = 8
WIDTH = 64
GROUP = HEADS // KV_HEADS
LANES = 2 * WIDTH
ROPE_BASE = 150000.0
LOG2_E = 1.4426950408889634
PAD_ROWS = 48
QUERY_BLOCK = 32
KEY_BLOCK = 1024
ROLL = ("yh", "z", "x")
SEQ = ("yl", "co")


def lane_frequencies(lanes):
    half = WIDTH // 2
    freq = ROPE_BASE ** (-(jnp.arange(half).astype(jnp.float32) * 2.0 / WIDTH))
    return jnp.tile(freq, lanes // half)


def ring(size, step):
    return [(i, (i + step) % size) for i in range(size)]


def reorder_kernel(source_ref, hidden_ref, out_ref):
    depth = hidden_ref.shape[1]
    index = lax.broadcasted_iota(jnp.int32, (depth, source_ref.shape[1]), 0)
    pick = jnp.where(index == source_ref[...], 1.0, 0.0).astype(jnp.bfloat16)
    out_ref[...] = jnp.dot(
        hidden_ref[...], pick, preferred_element_type=jnp.float32
    ).astype(jnp.bfloat16)


def reorder(hidden, source):
    rows, depth = hidden.shape
    columns = source.shape[1]
    tile = 256
    return pl.pallas_call(
        reorder_kernel,
        grid=(columns // tile,),
        in_specs=[
            pl.BlockSpec((1, tile), lambda i: (0, i)),
            pl.BlockSpec((rows, depth), lambda i: (0, 0)),
        ],
        out_specs=pl.BlockSpec((rows, tile), lambda i: (0, i)),
        out_shape=jax.ShapeDtypeStruct((rows, columns), jnp.bfloat16),
        name="reorder_hidden",
    )(source, hidden)


def swap_halves(x, lane):
    half = WIDTH // 2
    return jnp.where(
        lane % WIDTH < half,
        pltpu.roll(x, LANES - half, 1),
        pltpu.roll(x, half, 1),
    )


def product(hidden_ref, pieces):
    total, offset = None, 0
    for piece in pieces:
        size = piece.shape[0]
        part = jnp.dot(
            hidden_ref[:, offset : offset + size],
            piece[...],
            preferred_element_type=jnp.float32,
        )
        total = part if total is None else total + part
        offset += size
    return total


def first_half_kernel(core_ref, own_ref, other_ref, *rest):
    pieces, out_ref = rest[:-1], rest[-1]
    rows = own_ref.shape[0]
    core = core_ref[0]
    for hidden_ref, place in ((own_ref, core), (other_ref, 1 - core)):
        out_ref[pl.ds(pl.multiple_of(place * rows, rows), rows), :] = product(
            hidden_ref, pieces
        )


def first_half(core, own, other, pieces):
    vmem = pl.BlockSpec(memory_space=pltpu.VMEM)
    depth = sum(piece.shape[0] for piece in pieces)
    part = pl.BlockSpec((own.shape[0], depth), lambda i: (0, 0))
    return pl.pallas_call(
        first_half_kernel,
        grid=(1,),
        in_specs=[pl.BlockSpec(memory_space=pltpu.SMEM), part, part] + [vmem] * len(pieces),
        out_specs=vmem,
        out_shape=jax.ShapeDtypeStruct((2 * own.shape[0], pieces[0].shape[1]), jnp.float32),
        name="first_half",
    )(core, own, other, *pieces)


def project_kernel(core_ref, own_ref, other_ref, total_ref, cos_ref, sin_ref, *rest):
    pieces, out_ref = rest[:-1], rest[-1]
    rows = own_ref.shape[0]
    core = core_ref[0]
    lane = lax.broadcasted_iota(jnp.int32, (rows, LANES), 1)
    for hidden_ref, place in ((own_ref, core), (other_ref, 1 - core)):
        here = pl.ds(pl.multiple_of(place * rows, rows), rows)
        total = total_ref[here, :] + product(hidden_ref, pieces)
        cosine = cos_ref[here, :]
        sine = sin_ref[here, :]
        for head in range(out_ref.shape[0]):
            x = total[:, head * LANES : (head + 1) * LANES]
            out_ref[head, here, :] = (x * cosine + swap_halves(x, lane) * sine).astype(
                jnp.bfloat16
            )


def project(core, own, other, pieces, total, cosine, sine):
    rows = own.shape[0]
    heads = total.shape[1] // LANES
    vmem = pl.BlockSpec(memory_space=pltpu.VMEM)
    depth = sum(piece.shape[0] for piece in pieces)
    part = pl.BlockSpec((rows, depth), lambda i: (0, own.shape[1] // depth - 1))
    return pl.pallas_call(
        project_kernel,
        grid=(1,),
        in_specs=[pl.BlockSpec(memory_space=pltpu.SMEM), part, part]
        + [vmem] * (3 + len(pieces)),
        out_specs=vmem,
        out_shape=jax.ShapeDtypeStruct((heads, 2 * rows, LANES), jnp.bfloat16),
        name="project",
    )(core, own, other, total, cosine, sine, *pieces)


def prepare_kernel(query_ref, pick_ref, cos_ref, sin_ref, out_ref):
    rows = query_ref.shape[0]
    lane = lax.broadcasted_iota(jnp.int32, (rows, LANES), 1)
    pick = pick_ref[...]
    for pair in range(GROUP // 2):
        x = jnp.dot(
            pick,
            query_ref[:, pair * LANES : (pair + 1) * LANES],
            preferred_element_type=jnp.float32,
        )
        x = x * cos_ref[...] + swap_halves(x, lane) * sin_ref[...]
        x = x.astype(jnp.bfloat16).astype(jnp.float32) * (1.0 / 8.0)
        first = jnp.where(lane < WIDTH, x, 0.0).astype(jnp.bfloat16)
        second = jnp.where(lane < WIDTH, pltpu.roll(x, WIDTH, 1), 0.0).astype(jnp.bfloat16)
        for block in range(rows // QUERY_BLOCK):
            here = slice(block * QUERY_BLOCK, (block + 1) * QUERY_BLOCK)
            for head, value in ((2 * pair, first), (2 * pair + 1, second)):
                out_ref[block, head * QUERY_BLOCK : (head + 1) * QUERY_BLOCK, :] = value[here]


def prepare(query, pick, cosine, sine):
    rows = query.shape[0]
    vmem = pl.BlockSpec(memory_space=pltpu.VMEM)
    return pl.pallas_call(
        prepare_kernel,
        in_specs=[vmem] * 4,
        out_specs=vmem,
        out_shape=jax.ShapeDtypeStruct(
            (rows // QUERY_BLOCK, GROUP * QUERY_BLOCK, LANES), jnp.bfloat16
        ),
        name="prepare_queries",
    )(query, pick, cosine, sine)


def attend_kernel(
    bound_ref, query_ref, kv_ref, last_ref, unpick_ref, out_ref, value_ref, score_ref, sorted_ref
):
    blocks = query_ref.shape[0]
    rows = query_ref.shape[1]
    keys = kv_ref.shape[0]
    lane_kv = lax.broadcasted_iota(jnp.int32, (KEY_BLOCK, LANES), 1)
    for step in range(keys // KEY_BLOCK):
        here = slice(step * KEY_BLOCK, (step + 1) * KEY_BLOCK)
        value_ref[:, here] = jnp.where(
            lane_kv < WIDTH, 1.0, kv_ref[here, :].astype(jnp.float32)
        ).T.astype(jnp.bfloat16)
    key_index = lax.broadcasted_iota(jnp.int32, (KEY_BLOCK, rows), 0)
    lane = lax.broadcasted_iota(jnp.int32, (QUERY_BLOCK, LANES), 1)

    def one_block(block, carry):
        query = query_ref[block]
        last = last_ref[block]
        full, count = bound_ref[0, block], bound_ref[1, block]

        def score(masked, index, top):
            base = pl.multiple_of(index * KEY_BLOCK, KEY_BLOCK)
            scores = lax.dot_general(
                kv_ref[pl.ds(base, KEY_BLOCK), :],
                query,
                (((1,), (1,)), ((), ())),
                preferred_element_type=jnp.float32,
            )
            scores = scores * LOG2_E
            if masked:
                scores = jnp.where(key_index <= last - base, scores, -1e30)
            score_ref[pl.ds(base, KEY_BLOCK), :] = scores
            return jnp.maximum(top, jnp.max(scores.reshape(-1, 8, rows), axis=0))

        top = jnp.full((8, rows), -1e30, jnp.float32)
        top = lax.fori_loop(0, full, functools.partial(score, False), top)
        top = lax.fori_loop(full, count, functools.partial(score, True), top)
        top = jnp.max(top, axis=0, keepdims=True)

        def weigh(index, total):
            base = pl.multiple_of(index * KEY_BLOCK, KEY_BLOCK)
            expo = jnp.exp2(score_ref[pl.ds(base, KEY_BLOCK), :] - top)
            return total + jnp.dot(
                value_ref[:, pl.ds(base, KEY_BLOCK)],
                expo.astype(jnp.bfloat16),
                preferred_element_type=jnp.float32,
            )

        total = lax.fori_loop(0, count, weigh, jnp.zeros((LANES, rows), jnp.float32))
        result = total[WIDTH:] / total[:WIDTH]
        result = jnp.concatenate([result, result], 0).T
        place = pl.multiple_of(block * QUERY_BLOCK, QUERY_BLOCK)
        for pair in range(GROUP // 2):
            even = result[2 * pair * QUERY_BLOCK : (2 * pair + 1) * QUERY_BLOCK]
            odd = result[(2 * pair + 1) * QUERY_BLOCK : (2 * pair + 2) * QUERY_BLOCK]
            sorted_ref[pl.ds(place, QUERY_BLOCK), pair * LANES : (pair + 1) * LANES] = jnp.where(
                lane < WIDTH, even, odd
            ).astype(jnp.bfloat16)
        return carry

    lax.fori_loop(0, blocks, one_block, 0)
    out_ref[...] = jnp.dot(
        unpick_ref[...], sorted_ref[...], preferred_element_type=jnp.float32
    ).astype(jnp.bfloat16)


def attend(bounds, query, kv, last, unpick):
    vmem = pl.BlockSpec(memory_space=pltpu.VMEM)
    count = unpick.shape[0]
    keys = kv.shape[0]
    return pl.pallas_call(
        attend_kernel,
        in_specs=[pl.BlockSpec(memory_space=pltpu.SMEM)] + [vmem] * 4,
        out_specs=vmem,
        out_shape=jax.ShapeDtypeStruct((count, GROUP * WIDTH), jnp.bfloat16),
        scratch_shapes=[
            pltpu.VMEM((LANES, keys), jnp.bfloat16),
            pltpu.VMEM((keys, query.shape[1]), jnp.float32),
            pltpu.VMEM((count, GROUP * WIDTH), jnp.bfloat16),
        ],
        name="attend",
    )(bounds, query, kv, last, unpick)


def spread(x, axis):
    size = lax.axis_size(axis)
    copies = jnp.broadcast_to(x[None], (size,) + x.shape)
    whole = lax.all_to_all(copies, axis, 0, 0, tiled=True)
    return whole.reshape((-1,) + x.shape[1:])


def gather_weight(blocks):
    block_rows = blocks.shape[0]
    core = lax.axis_index("co")
    split = blocks.reshape(block_rows, KV_HEADS // 2, 2, LANES)
    mine = lax.dynamic_index_in_dim(split, core, 2, False).reshape(block_rows, -1)
    mine = jnp.pad(mine, ((0, PAD_ROWS - block_rows), (0, 0)))
    plane = spread(mine, ("yh", "z"))
    half = plane.shape[0] // 2
    up, down = ring(4, 1), ring(4, -1)
    below = lax.ppermute(plane, "x", up)
    above = lax.ppermute(plane, "x", down)
    low = lax.ppermute(below[:half], "x", up)
    high = lax.ppermute(above[half:], "x", down)
    return (plane, below, above), (low, high)


def slot_order(block_of):
    x = lax.axis_index("x")
    xs = jnp.stack([x, x + 3, x + 1, x + 2]) % 4
    stored = jnp.arange(16)[None, :] * 4 + xs[:, None]
    return block_of[stored.reshape(-1)]


def attention(hidden, blocks, block_of, queries, key_pos, query_pos):
    core = lax.axis_index("co")
    seq_index = lax.axis_index(SEQ)
    seq = lax.axis_size(SEQ)
    rows = hidden.shape[1]
    keys = rows * seq
    block_rows = blocks.shape[0]
    query_rows = queries.shape[1]
    start = key_pos[0, 0] - rows * seq_index

    slots = slot_order(block_of)
    inner = jnp.arange(PAD_ROWS)
    source = jnp.where(
        inner[None, :] < block_rows, slots[:, None] * block_rows + inner[None, :], -1
    ).reshape(1, -1)

    high = (query_pos[0] >> 8).astype(jnp.bfloat16)
    low = (query_pos[0] & 255).astype(jnp.bfloat16)
    extra = jnp.concatenate(
        [
            jnp.broadcast_to(high[:, None, None], (query_rows, KV_HEADS, WIDTH)),
            jnp.broadcast_to(low[:, None, None], (query_rows, KV_HEADS, WIDTH)),
        ],
        -1,
    )
    payload = jnp.concatenate([queries[0].reshape(query_rows, KV_HEADS, GROUP * WIDTH), extra], -1)
    payload = lax.all_to_all(payload.transpose(1, 0, 2), SEQ, 0, 0, tiled=True)

    near, far = gather_weight(blocks)
    own = reorder(hidden[0], source)
    other = lax.ppermute(own, "co", ring(2, 1))

    total_queries = query_rows * seq
    payload = payload.reshape(total_queries, -1)
    query = payload[:, : GROUP * WIDTH]
    positions = (
        payload[:, GROUP * WIDTH].astype(jnp.float32) * 256.0
        + payload[:, GROUP * WIDTH + WIDTH].astype(jnp.float32)
    ).astype(jnp.int32)
    order = jnp.arange(total_queries)
    before = (positions[None, :] < positions[:, None]) | (
        (positions[None, :] == positions[:, None]) & (order[None, :] < order[:, None])
    )
    rank = jnp.sum(before.astype(jnp.int32), axis=1)
    pick_mask = rank[None, :] == order[:, None]
    sorted_pos = jnp.sum(jnp.where(pick_mask, positions[None, :], 0), axis=1)
    pick = pick_mask.astype(jnp.bfloat16)
    unpick = (rank[:, None] == order[None, :]).astype(jnp.bfloat16)
    last = sorted_pos - start
    by_block = last.reshape(-1, QUERY_BLOCK)
    bounds = jnp.stack([(by_block[:, 0] + 1) // KEY_BLOCK, by_block[:, -1] // KEY_BLOCK + 1])
    last_rows = jnp.tile(by_block, (1, GROUP))[:, None, :]

    sign = jnp.asarray(np.where(np.arange(LANES) % WIDTH < WIDTH // 2, -1.0, 1.0), jnp.float32)
    freq = lane_frequencies(LANES)
    query_angle = sorted_pos.astype(jnp.float32)[:, None] * freq[None, :]
    prepared = prepare(query, pick, jnp.cos(query_angle), jnp.sin(query_angle) * sign)

    is_key = jnp.arange(LANES) < WIDTH
    chip_rows = 2 * rows
    chip_pos = start + chip_rows * lax.axis_index("yl") + jnp.arange(chip_rows)
    key_angle = chip_pos.astype(jnp.float32)[:, None] * jnp.where(is_key, freq, 0.0)[None, :]
    key_sine = jnp.sin(key_angle) * jnp.where(is_key, sign, 0.0)

    place = core.reshape(1)
    total = first_half(place, own, other, near)
    kv = project(place, own, other, far, total, jnp.cos(key_angle), key_sine)
    kv = lax.all_to_all(kv, "yl", 0, 0, tiled=True).reshape(keys, LANES)
    context = attend(bounds, prepared, kv, last_rows, unpick)
    context = context.reshape(seq, query_rows, GROUP * WIDTH)
    context = lax.all_to_all(context, SEQ, 0, 0, tiled=True)
    return context.transpose(1, 0, 2).reshape(1, query_rows, HEADS * WIDTH)


def solution(mesh):
    fine = Mesh(mesh.devices.reshape(2, 8, 4, 4, 2), ROLL + SEQ)
    return jax.shard_map(
        attention,
        mesh=fine,
        in_specs=(
            P(ROLL, SEQ, None),
            P(ROLL, None),
            P(),
            P(ROLL, SEQ, None),
            P(ROLL, SEQ),
            P(ROLL, SEQ),
        ),
        out_specs=P(ROLL, SEQ, None),
        check_vma=False,
    )
```

```python
import functools

import jax
import jax.numpy as jnp
import numpy as np
from jax import lax
from jax.experimental import pallas as pl
from jax.experimental.pallas import tpu as pltpu
from jax.sharding import Mesh, PartitionSpec as P


HEADS = 64
KV_HEADS = 8
WIDTH = 64
GROUP = HEADS // KV_HEADS
LANES = 2 * WIDTH
ROPE_BASE = 150000.0
LOG2_E = 1.4426950408889634
PAD_ROWS = 48
QUERY_BLOCK = 32
KEY_BLOCK = 1024
ROLL = ("yh", "z", "x")
SEQ = ("yl", "co")


def lane_frequencies(lanes):
    half = WIDTH // 2
    freq = ROPE_BASE ** (-(jnp.arange(half).astype(jnp.float32) * 2.0 / WIDTH))
    return jnp.tile(freq, lanes // half)


def ring(size, step):
    return [(i, (i + step) % size) for i in range(size)]


def reorder_kernel(source_ref, hidden_ref, out_ref):
    depth = hidden_ref.shape[1]
    index = lax.broadcasted_iota(jnp.int32, (depth, source_ref.shape[1]), 0)
    pick = jnp.where(index == source_ref[...], 1.0, 0.0).astype(jnp.bfloat16)
    out_ref[...] = jnp.dot(
        hidden_ref[...], pick, preferred_element_type=jnp.float32
    ).astype(jnp.bfloat16)


def reorder(hidden, source):
    rows, depth = hidden.shape
    columns = source.shape[1]
    tile = 256
    return pl.pallas_call(
        reorder_kernel,
        grid=(columns // tile,),
        in_specs=[
            pl.BlockSpec((1, tile), lambda i: (0, i)),
            pl.BlockSpec((rows, depth), lambda i: (0, 0)),
        ],
        out_specs=pl.BlockSpec((rows, tile), lambda i: (0, i)),
        out_shape=jax.ShapeDtypeStruct((rows, columns), jnp.bfloat16),
        name="reorder_hidden",
        compiler_params=pltpu.CompilerParams(vmem_limit_bytes=16 << 20),
    )(source, hidden)


def swap_halves(x, lane):
    half = WIDTH // 2
    return jnp.where(
        lane % WIDTH < half,
        pltpu.roll(x, LANES - half, 1),
        pltpu.roll(x, half, 1),
    )


def product(hidden_ref, pieces):
    total, offset = None, 0
    for piece in pieces:
        size = piece.shape[0]
        part = jnp.dot(
            hidden_ref[:, offset : offset + size],
            piece[...],
            preferred_element_type=jnp.float32,
        )
        total = part if total is None else total + part
        offset += size
    return total


def first_half_kernel(core_ref, own_ref, other_ref, *rest):
    pieces, out_ref = rest[:-1], rest[-1]
    rows = own_ref.shape[0]
    core = core_ref[0]
    for hidden_ref, place in ((own_ref, core), (other_ref, 1 - core)):
        out_ref[pl.ds(pl.multiple_of(place * rows, rows), rows), :] = product(
            hidden_ref, pieces
        )


def first_half(core, own, other, pieces):
    vmem = pl.BlockSpec(memory_space=pltpu.VMEM)
    depth = sum(piece.shape[0] for piece in pieces)
    part = pl.BlockSpec((own.shape[0], depth), lambda i: (0, 0))
    return pl.pallas_call(
        first_half_kernel,
        grid=(1,),
        in_specs=[pl.BlockSpec(memory_space=pltpu.SMEM), part, part] + [vmem] * len(pieces),
        out_specs=vmem,
        out_shape=jax.ShapeDtypeStruct((2 * own.shape[0], pieces[0].shape[1]), jnp.float32),
        name="first_half",
        compiler_params=pltpu.CompilerParams(vmem_limit_bytes=20 << 20),
    )(core, own, other, *pieces)


def project_kernel(core_ref, own_ref, other_ref, total_ref, cos_ref, sin_ref, *rest):
    pieces, out_ref = rest[:-1], rest[-1]
    rows = own_ref.shape[0]
    core = core_ref[0]
    lane = lax.broadcasted_iota(jnp.int32, (rows, LANES), 1)
    for hidden_ref, place in ((own_ref, core), (other_ref, 1 - core)):
        here = pl.ds(pl.multiple_of(place * rows, rows), rows)
        total = total_ref[here, :] + product(hidden_ref, pieces)
        cosine = cos_ref[here, :]
        sine = sin_ref[here, :]
        for head in range(out_ref.shape[0]):
            x = total[:, head * LANES : (head + 1) * LANES]
            out_ref[head, here, :] = (x * cosine + swap_halves(x, lane) * sine).astype(
                jnp.bfloat16
            )


def project(core, own, other, pieces, total, cosine, sine):
    rows = own.shape[0]
    heads = total.shape[1] // LANES
    vmem = pl.BlockSpec(memory_space=pltpu.VMEM)
    depth = sum(piece.shape[0] for piece in pieces)
    part = pl.BlockSpec((rows, depth), lambda i: (0, own.shape[1] // depth - 1))
    return pl.pallas_call(
        project_kernel,
        grid=(1,),
        in_specs=[pl.BlockSpec(memory_space=pltpu.SMEM), part, part]
        + [vmem] * (3 + len(pieces)),
        out_specs=vmem,
        out_shape=jax.ShapeDtypeStruct((heads, 2 * rows, LANES), jnp.bfloat16),
        name="project",
        compiler_params=pltpu.CompilerParams(vmem_limit_bytes=20 << 20),
    )(core, own, other, total, cosine, sine, *pieces)


def prepare_kernel(query_ref, pick_ref, cos_ref, sin_ref, out_ref):
    rows = query_ref.shape[0]
    lane = lax.broadcasted_iota(jnp.int32, (rows, LANES), 1)
    pick = pick_ref[...]
    for pair in range(GROUP // 2):
        x = jnp.dot(
            pick,
            query_ref[:, pair * LANES : (pair + 1) * LANES],
            preferred_element_type=jnp.float32,
        )
        x = x * cos_ref[...] + swap_halves(x, lane) * sin_ref[...]
        x = x.astype(jnp.bfloat16).astype(jnp.float32) * (1.0 / 8.0)
        first = jnp.where(lane < WIDTH, x, 0.0).astype(jnp.bfloat16)
        second = jnp.where(lane < WIDTH, pltpu.roll(x, WIDTH, 1), 0.0).astype(jnp.bfloat16)
        for block in range(rows // QUERY_BLOCK):
            here = slice(block * QUERY_BLOCK, (block + 1) * QUERY_BLOCK)
            for head, value in ((2 * pair, first), (2 * pair + 1, second)):
                out_ref[block, head * QUERY_BLOCK : (head + 1) * QUERY_BLOCK, :] = value[here]


def prepare(query, pick, cosine, sine):
    rows = query.shape[0]
    vmem = pl.BlockSpec(memory_space=pltpu.VMEM)
    return pl.pallas_call(
        prepare_kernel,
        in_specs=[vmem] * 4,
        out_specs=vmem,
        out_shape=jax.ShapeDtypeStruct(
            (rows // QUERY_BLOCK, GROUP * QUERY_BLOCK, LANES), jnp.bfloat16
        ),
        name="prepare_queries",
        compiler_params=pltpu.CompilerParams(vmem_limit_bytes=6 << 20),
    )(query, pick, cosine, sine)


def attend_kernel(
    bound_ref, query_ref, kv_ref, last_ref, unpick_ref, out_ref, value_ref, even_ref, odd_ref, sorted_ref
):
    blocks = query_ref.shape[0]
    rows = query_ref.shape[1]
    keys = kv_ref.shape[0]
    value_ref[WIDTH:, :] = jnp.ones((value_ref.shape[0] - WIDTH, keys), jnp.bfloat16)
    for step in range(keys // KEY_BLOCK):
        here = slice(step * KEY_BLOCK, (step + 1) * KEY_BLOCK)
        value_ref[:WIDTH, here] = kv_ref[here, :].T[WIDTH:]
    key_index = lax.broadcasted_iota(jnp.int32, (KEY_BLOCK, rows), 0)
    lane = lax.broadcasted_iota(jnp.int32, (QUERY_BLOCK, LANES), 1)
    no_top = jnp.full((8, rows), -1e30, jnp.float32)
    no_total = jnp.zeros((value_ref.shape[0], rows), jnp.float32)

    def score(score_ref, block, masked, index, top):
        base = pl.multiple_of(index * KEY_BLOCK, KEY_BLOCK)
        scores = lax.dot_general(
            kv_ref[pl.ds(base, KEY_BLOCK), :],
            query_ref[block],
            (((1,), (1,)), ((), ())),
            preferred_element_type=jnp.float32,
        )
        scores = scores * LOG2_E
        if masked:
            scores = jnp.where(key_index <= last_ref[block] - base, scores, -1e30)
        score_ref[pl.ds(base, KEY_BLOCK), :] = scores
        return jnp.maximum(top, jnp.max(scores.reshape(-1, 8, rows), axis=0))

    def weigh(score_ref, top, index, total):
        base = pl.multiple_of(index * KEY_BLOCK, KEY_BLOCK)
        expo = jnp.exp2(score_ref[pl.ds(base, KEY_BLOCK), :] - top)
        return total + jnp.dot(
            value_ref[:, pl.ds(base, KEY_BLOCK)],
            expo.astype(jnp.bfloat16),
            preferred_element_type=jnp.float32,
        )

    def score_range(score_ref, block, begin, top):
        full, count = bound_ref[0, block], bound_ref[1, block]
        middle = jnp.maximum(begin, full)
        top = lax.fori_loop(
            begin, middle, functools.partial(score, score_ref, block, False), top
        )
        return lax.fori_loop(
            middle, count, functools.partial(score, score_ref, block, True), top
        )

    def finish(block, total):
        result = total[:WIDTH] / total[WIDTH : WIDTH + 1]
        result = jnp.concatenate([result, result], 0).T
        place = pl.multiple_of(block * QUERY_BLOCK, QUERY_BLOCK)
        for pair in range(GROUP // 2):
            even = result[2 * pair * QUERY_BLOCK : (2 * pair + 1) * QUERY_BLOCK]
            odd = result[(2 * pair + 1) * QUERY_BLOCK : (2 * pair + 2) * QUERY_BLOCK]
            sorted_ref[pl.ds(place, QUERY_BLOCK), pair * LANES : (pair + 1) * LANES] = jnp.where(
                lane < WIDTH, even, odd
            ).astype(jnp.bfloat16)

    def one_block(here_ref, next_ref, block, top):
        top = jnp.max(top, axis=0, keepdims=True)
        count = bound_ref[1, block]
        middle = jnp.minimum(count, bound_ref[0, block + 1])

        def both(masked, index, state):
            next_top, total = state
            return (
                score(next_ref, block + 1, masked, index, next_top),
                weigh(here_ref, top, index, total),
            )

        state = lax.fori_loop(0, middle, functools.partial(both, False), (no_top, no_total))
        state = lax.fori_loop(middle, count, functools.partial(both, True), state)
        finish(block, state[1])
        return score_range(next_ref, block + 1, count, state[0])

    def two_blocks(pair, top):
        top = one_block(even_ref, odd_ref, 2 * pair, top)
        return one_block(odd_ref, even_ref, 2 * pair + 1, top)

    top = score_range(even_ref, 0, 0, no_top)
    top = lax.fori_loop(0, blocks // 2 - 1, two_blocks, top)
    top = one_block(even_ref, odd_ref, blocks - 2, top)
    top = jnp.max(top, axis=0, keepdims=True)
    final = blocks - 1
    total = lax.fori_loop(
        0, bound_ref[1, final], functools.partial(weigh, odd_ref, top), no_total
    )
    finish(final, total)
    out_ref[...] = jnp.dot(
        unpick_ref[...], sorted_ref[...], preferred_element_type=jnp.float32
    ).astype(jnp.bfloat16)


def attend(bounds, query, kv, last, unpick):
    vmem = pl.BlockSpec(memory_space=pltpu.VMEM)
    count = unpick.shape[0]
    keys = kv.shape[0]
    return pl.pallas_call(
        attend_kernel,
        in_specs=[pl.BlockSpec(memory_space=pltpu.SMEM)] + [vmem] * 4,
        out_specs=vmem,
        out_shape=jax.ShapeDtypeStruct((count, GROUP * WIDTH), jnp.bfloat16),
        scratch_shapes=[
            pltpu.VMEM((WIDTH + 16, keys), jnp.bfloat16),
            pltpu.VMEM((keys, query.shape[1]), jnp.float32),
            pltpu.VMEM((keys, query.shape[1]), jnp.float32),
            pltpu.VMEM((count, GROUP * WIDTH), jnp.bfloat16),
        ],
        name="attend",
        compiler_params=pltpu.CompilerParams(vmem_limit_bytes=18 << 20),
    )(bounds, query, kv, last, unpick)


def spread(x, axis):
    size = lax.axis_size(axis)
    copies = jnp.broadcast_to(x[None], (size,) + x.shape)
    whole = lax.all_to_all(copies, axis, 0, 0, tiled=True)
    return whole.reshape((-1,) + x.shape[1:])


def gather_weight(blocks):
    block_rows = blocks.shape[0]
    core = lax.axis_index("co")
    split = blocks.reshape(block_rows, KV_HEADS // 2, 2, LANES)
    mine = lax.dynamic_index_in_dim(split, core, 2, False).reshape(block_rows, -1)
    mine = jnp.pad(mine, ((0, PAD_ROWS - block_rows), (0, 0)))
    plane = spread(mine, ("yh", "z"))
    half = plane.shape[0] // 2
    up, down = ring(4, 1), ring(4, -1)
    below = lax.ppermute(plane, "x", up)
    above = lax.ppermute(plane, "x", down)
    low = lax.ppermute(below[:half], "x", up)
    high = lax.ppermute(above[half:], "x", down)
    return (plane, below, above), (low, high)


def slot_order(block_of):
    x = lax.axis_index("x")
    xs = jnp.stack([x, x + 3, x + 1, x + 2]) % 4
    stored = jnp.arange(16)[None, :] * 4 + xs[:, None]
    return block_of[stored.reshape(-1)]


def attention(hidden, blocks, block_of, queries, key_pos, query_pos):
    core = lax.axis_index("co")
    seq_index = lax.axis_index(SEQ)
    seq = lax.axis_size(SEQ)
    rows = hidden.shape[1]
    keys = rows * seq
    block_rows = blocks.shape[0]
    query_rows = queries.shape[1]
    start = key_pos[0, 0] - rows * seq_index

    slots = slot_order(block_of)
    inner = jnp.arange(PAD_ROWS)
    source = jnp.where(
        inner[None, :] < block_rows, slots[:, None] * block_rows + inner[None, :], -1
    ).reshape(1, -1)

    high = (query_pos[0] >> 8).astype(jnp.bfloat16)
    low = (query_pos[0] & 255).astype(jnp.bfloat16)
    extra = jnp.concatenate(
        [
            jnp.broadcast_to(high[:, None, None], (query_rows, KV_HEADS, WIDTH)),
            jnp.broadcast_to(low[:, None, None], (query_rows, KV_HEADS, WIDTH)),
        ],
        -1,
    )
    payload = jnp.concatenate([queries[0].reshape(query_rows, KV_HEADS, GROUP * WIDTH), extra], -1)
    payload = lax.all_to_all(payload.transpose(1, 0, 2), SEQ, 0, 0, tiled=True)

    sign = jnp.asarray(np.where(np.arange(LANES) % WIDTH < WIDTH // 2, -1.0, 1.0), jnp.float32)
    freq = lane_frequencies(LANES)
    is_key = jnp.arange(LANES) < WIDTH
    chip_rows = 2 * rows
    chip_pos = start + chip_rows * lax.axis_index("yl") + jnp.arange(chip_rows)
    key_angle = chip_pos.astype(jnp.float32)[:, None] * jnp.where(is_key, freq, 0.0)[None, :]
    key_cosine = jnp.cos(key_angle)
    key_sine = jnp.sin(key_angle) * jnp.where(is_key, sign, 0.0)
    near, far = gather_weight(blocks)
    own = reorder(hidden[0], source)
    other = lax.ppermute(own, "co", ring(2, 1))

    total_queries = query_rows * seq
    payload = payload.reshape(total_queries, -1)
    query = payload[:, : GROUP * WIDTH]
    positions = (
        payload[:, GROUP * WIDTH].astype(jnp.float32) * 256.0
        + payload[:, GROUP * WIDTH + WIDTH].astype(jnp.float32)
    ).astype(jnp.int32)
    order = jnp.arange(total_queries)
    before = (positions[None, :] < positions[:, None]) | (
        (positions[None, :] == positions[:, None]) & (order[None, :] < order[:, None])
    )
    rank = jnp.sum(before.astype(jnp.int32), axis=1)
    pick_mask = rank[None, :] == order[:, None]
    sorted_pos = jnp.sum(jnp.where(pick_mask, positions[None, :], 0), axis=1)
    pick = pick_mask.astype(jnp.bfloat16)
    unpick = (rank[:, None] == order[None, :]).astype(jnp.bfloat16)
    last = sorted_pos - start
    by_block = last.reshape(-1, QUERY_BLOCK)
    bounds = jnp.stack([(by_block[:, 0] + 1) // KEY_BLOCK, by_block[:, -1] // KEY_BLOCK + 1])
    last_rows = jnp.tile(by_block, (1, GROUP))[:, None, :]

    query_angle = sorted_pos.astype(jnp.float32)[:, None] * freq[None, :]
    prepared = prepare(query, pick, jnp.cos(query_angle), jnp.sin(query_angle) * sign)

    place = core.reshape(1)
    total = first_half(place, own, other, near)
    kv = project(place, own, other, far, total, key_cosine, key_sine)
    kv = lax.all_to_all(kv, "yl", 0, 0, tiled=True).reshape(keys, LANES)
    context = attend(bounds, prepared, kv, last_rows, unpick)
    context = context.reshape(seq, query_rows, GROUP * WIDTH)
    context = lax.all_to_all(context, SEQ, 0, 0, tiled=True)
    return context.transpose(1, 0, 2).reshape(1, query_rows, HEADS * WIDTH)


def solution(mesh):
    fine = Mesh(mesh.devices.reshape(2, 8, 4, 4, 2), ROLL + SEQ)
    return jax.shard_map(
        attention,
        mesh=fine,
        in_specs=(
            P(ROLL, SEQ, None),
            P(ROLL, None),
            P(),
            P(ROLL, SEQ, None),
            P(ROLL, SEQ),
            P(ROLL, SEQ),
        ),
        out_specs=P(ROLL, SEQ, None),
        check_vma=False,
    )
```

```python
import functools

import jax
import jax.numpy as jnp
import numpy as np
from jax import lax
from jax.experimental import pallas as pl
from jax.experimental.pallas import tpu as pltpu
from jax.sharding import Mesh, PartitionSpec as P


HEADS = 64
KV_HEADS = 8
WIDTH = 64
GROUP = HEADS // KV_HEADS
LANES = 2 * WIDTH
ROPE_BASE = 150000.0
LOG2_E = 1.4426950408889634
PAD_ROWS = 48
QUERY_BLOCK = 32
KEY_BLOCK = 1024
ROLL = ("yh", "z", "x")
SEQ = ("yl", "co")


def lane_frequencies(lanes):
    half = WIDTH // 2
    freq = ROPE_BASE ** (-(jnp.arange(half).astype(jnp.float32) * 2.0 / WIDTH))
    return jnp.tile(freq, lanes // half)


def ring(size, step):
    return [(i, (i + step) % size) for i in range(size)]


def reorder_kernel(window_ref, source_ref, hidden_ref, out_ref):
    group = pl.program_id(0)
    index = lax.broadcasted_iota(jnp.int32, (2 * LANES, LANES), 0)
    lane = lax.broadcasted_iota(jnp.int32, (1, LANES), 1)
    slots = out_ref.shape[1] // PAD_ROWS
    for tile in range(out_ref.shape[1] // LANES):
        begin = tile * LANES
        source = source_ref[:, begin : begin + LANES]
        rows, picks = [], []
        for slot in range(slots):
            low, high = slot * PAD_ROWS - begin, (slot + 1) * PAD_ROWS - begin
            if high <= 0 or low >= LANES:
                continue
            window = pl.multiple_of(window_ref[group * slots + slot], LANES)
            place = jnp.where((lane >= low) & (lane < high), source - window, -1)
            picks.append(jnp.where(index == place, 1.0, 0.0).astype(jnp.bfloat16))
            rows.append(hidden_ref[:, pl.ds(window, 2 * LANES)])
        out_ref[:, begin : begin + LANES] = jnp.dot(
            jnp.concatenate(rows, 1),
            jnp.concatenate(picks, 0),
            preferred_element_type=jnp.float32,
        ).astype(jnp.bfloat16)


def reorder(hidden, source, window):
    rows, depth = hidden.shape
    columns = source.shape[1]
    tile = 8 * PAD_ROWS
    return pl.pallas_call(
        reorder_kernel,
        grid=(columns // tile,),
        in_specs=[
            pl.BlockSpec(memory_space=pltpu.SMEM),
            pl.BlockSpec((1, tile), lambda i: (0, i)),
            pl.BlockSpec((rows, depth), lambda i: (0, 0)),
        ],
        out_specs=pl.BlockSpec((rows, tile), lambda i: (0, i)),
        out_shape=jax.ShapeDtypeStruct((rows, columns), jnp.bfloat16),
        name="reorder_hidden",
        compiler_params=pltpu.CompilerParams(vmem_limit_bytes=16 << 20),
    )(window, source, hidden)


def swap_halves(x, lane):
    half = WIDTH // 2
    return jnp.where(
        lane % WIDTH < half,
        pltpu.roll(x, LANES - half, 1),
        pltpu.roll(x, half, 1),
    )


def product(hidden_ref, pieces):
    weight = jnp.concatenate([piece[...] for piece in pieces], 0)
    return jnp.dot(hidden_ref[...], weight, preferred_element_type=jnp.float32)


def partial_kernel(core_ref, own_ref, other_ref, *rest):
    pieces, out_ref = rest[:-1], rest[-1]
    rows = own_ref.shape[0]
    core = core_ref[0]
    for hidden_ref, place in ((own_ref, core), (other_ref, 1 - core)):
        here = pl.ds(pl.multiple_of(place * rows, rows), rows)
        out_ref[here, :] = product(hidden_ref, pieces)


def partial_sum_kernel(core_ref, own_ref, other_ref, total_ref, *rest):
    pieces, out_ref = rest[:-1], rest[-1]
    rows = own_ref.shape[0]
    core = core_ref[0]
    for hidden_ref, place in ((own_ref, core), (other_ref, 1 - core)):
        here = pl.ds(pl.multiple_of(place * rows, rows), rows)
        out_ref[here, :] = total_ref[here, :] + product(hidden_ref, pieces)


def partial_product(core, own, other, pieces, *total):
    vmem = pl.BlockSpec(memory_space=pltpu.VMEM)
    rows = own.shape[0]
    column = 0 if total else 2
    part = pl.BlockSpec((rows, sum(p.shape[0] for p in pieces)), lambda i: (0, column))
    return pl.pallas_call(
        partial_sum_kernel if total else partial_kernel,
        grid=(1,),
        in_specs=[pl.BlockSpec(memory_space=pltpu.SMEM)]
        + [part, part]
        + [vmem] * (len(pieces) + len(total)),
        out_specs=vmem,
        out_shape=jax.ShapeDtypeStruct((2 * rows, pieces[0].shape[1]), jnp.float32),
        name="middle_product" if total else "first_product",
        compiler_params=pltpu.CompilerParams(vmem_limit_bytes=18 << 20),
    )(core, own, other, *total, *pieces)


def project_kernel(core_ref, own_ref, other_ref, total_ref, cos_ref, sin_ref, *rest):
    pieces, out_ref = rest[:-1], rest[-1]
    rows = own_ref.shape[0]
    core = core_ref[0]
    lane = lax.broadcasted_iota(jnp.int32, (rows, LANES), 1)
    for hidden_ref, place in ((own_ref, core), (other_ref, 1 - core)):
        here = pl.ds(pl.multiple_of(place * rows, rows), rows)
        total = total_ref[here, :] + product(hidden_ref, pieces)
        cosine = cos_ref[here, :]
        sine = sin_ref[here, :]
        for head in range(out_ref.shape[0]):
            x = total[:, head * LANES : (head + 1) * LANES]
            out_ref[head, here, :] = (x * cosine + swap_halves(x, lane) * sine).astype(
                jnp.bfloat16
            )


def project(core, own, other, pieces, total, cosine, sine):
    rows = own.shape[0]
    heads = total.shape[1] // LANES
    vmem = pl.BlockSpec(memory_space=pltpu.VMEM)
    depth = sum(piece.shape[0] for piece in pieces)
    part = pl.BlockSpec((rows, depth), lambda i: (0, own.shape[1] // depth - 1))
    return pl.pallas_call(
        project_kernel,
        grid=(1,),
        in_specs=[pl.BlockSpec(memory_space=pltpu.SMEM), part, part]
        + [vmem] * (3 + len(pieces)),
        out_specs=vmem,
        out_shape=jax.ShapeDtypeStruct((heads, 2 * rows, LANES), jnp.bfloat16),
        name="project",
        compiler_params=pltpu.CompilerParams(vmem_limit_bytes=20 << 20),
    )(core, own, other, total, cosine, sine, *pieces)


def prepare_kernel(query_ref, pick_ref, cos_ref, sin_ref, out_ref):
    rows = query_ref.shape[0]
    lane = lax.broadcasted_iota(jnp.int32, (rows, LANES), 1)
    pick = pick_ref[...]
    for pair in range(GROUP // 2):
        x = jnp.dot(
            pick,
            query_ref[:, pair * LANES : (pair + 1) * LANES],
            preferred_element_type=jnp.float32,
        )
        x = x * cos_ref[...] + swap_halves(x, lane) * sin_ref[...]
        x = x.astype(jnp.bfloat16).astype(jnp.float32) * (1.0 / 8.0)
        first = jnp.where(lane < WIDTH, x, 0.0).astype(jnp.bfloat16)
        second = jnp.where(lane < WIDTH, pltpu.roll(x, WIDTH, 1), 0.0).astype(jnp.bfloat16)
        for block in range(rows // QUERY_BLOCK):
            here = slice(block * QUERY_BLOCK, (block + 1) * QUERY_BLOCK)
            for head, value in ((2 * pair, first), (2 * pair + 1, second)):
                out_ref[block, head * QUERY_BLOCK : (head + 1) * QUERY_BLOCK, :] = value[here]


def prepare(query, pick, cosine, sine):
    rows = query.shape[0]
    vmem = pl.BlockSpec(memory_space=pltpu.VMEM)
    return pl.pallas_call(
        prepare_kernel,
        in_specs=[vmem] * 4,
        out_specs=vmem,
        out_shape=jax.ShapeDtypeStruct(
            (rows // QUERY_BLOCK, GROUP * QUERY_BLOCK, LANES), jnp.bfloat16
        ),
        name="prepare_queries",
        compiler_params=pltpu.CompilerParams(vmem_limit_bytes=6 << 20),
    )(query, pick, cosine, sine)


def attend_kernel(
    bound_ref, query_ref, kv_ref, last_ref, unpick_ref, out_ref, value_ref, even_ref, odd_ref, sorted_ref
):
    blocks = query_ref.shape[0]
    rows = query_ref.shape[1]
    keys = kv_ref.shape[0]
    value_ref[WIDTH:, :] = jnp.ones((value_ref.shape[0] - WIDTH, keys), jnp.bfloat16)
    for step in range(keys // KEY_BLOCK):
        here = slice(step * KEY_BLOCK, (step + 1) * KEY_BLOCK)
        value_ref[:WIDTH, here] = kv_ref[here, :].T[WIDTH:]
    key_index = lax.broadcasted_iota(jnp.int32, (KEY_BLOCK, rows), 0)
    lane = lax.broadcasted_iota(jnp.int32, (QUERY_BLOCK, LANES), 1)
    no_top = jnp.full((8, rows), -1e30, jnp.float32)
    no_total = jnp.zeros((value_ref.shape[0], rows), jnp.float32)

    def score(score_ref, block, masked, index, top):
        base = pl.multiple_of(index * KEY_BLOCK, KEY_BLOCK)
        scores = lax.dot_general(
            kv_ref[pl.ds(base, KEY_BLOCK), :],
            query_ref[block],
            (((1,), (1,)), ((), ())),
            preferred_element_type=jnp.float32,
        )
        scores = scores * LOG2_E
        if masked:
            scores = jnp.where(key_index <= last_ref[block] - base, scores, -1e30)
        score_ref[pl.ds(base, KEY_BLOCK), :] = scores
        return jnp.maximum(top, jnp.max(scores.reshape(-1, 8, rows), axis=0))

    def weigh(score_ref, top, index, total):
        base = pl.multiple_of(index * KEY_BLOCK, KEY_BLOCK)
        expo = jnp.exp2(score_ref[pl.ds(base, KEY_BLOCK), :] - top)
        return total + jnp.dot(
            value_ref[:, pl.ds(base, KEY_BLOCK)],
            expo.astype(jnp.bfloat16),
            preferred_element_type=jnp.float32,
        )

    def score_range(score_ref, block, begin, top):
        full, count = bound_ref[0, block], bound_ref[1, block]
        middle = jnp.maximum(begin, full)
        top = lax.fori_loop(
            begin, middle, functools.partial(score, score_ref, block, False), top
        )
        return lax.fori_loop(
            middle, count, functools.partial(score, score_ref, block, True), top
        )

    def finish(block, total):
        result = total[:WIDTH] / total[WIDTH : WIDTH + 1]
        result = jnp.concatenate([result, result], 0).T
        place = pl.multiple_of(block * QUERY_BLOCK, QUERY_BLOCK)
        for pair in range(GROUP // 2):
            even = result[2 * pair * QUERY_BLOCK : (2 * pair + 1) * QUERY_BLOCK]
            odd = result[(2 * pair + 1) * QUERY_BLOCK : (2 * pair + 2) * QUERY_BLOCK]
            sorted_ref[pl.ds(place, QUERY_BLOCK), pair * LANES : (pair + 1) * LANES] = jnp.where(
                lane < WIDTH, even, odd
            ).astype(jnp.bfloat16)

    def one_block(here_ref, next_ref, block, top):
        top = jnp.max(top, axis=0, keepdims=True)
        count = bound_ref[1, block]
        middle = jnp.minimum(count, bound_ref[0, block + 1])

        def both(masked, index, state):
            next_top, total = state
            return (
                score(next_ref, block + 1, masked, index, next_top),
                weigh(here_ref, top, index, total),
            )

        state = lax.fori_loop(0, middle, functools.partial(both, False), (no_top, no_total))
        state = lax.fori_loop(middle, count, functools.partial(both, True), state)
        finish(block, state[1])
        return score_range(next_ref, block + 1, count, state[0])

    def two_blocks(pair, top):
        top = one_block(even_ref, odd_ref, 2 * pair, top)
        return one_block(odd_ref, even_ref, 2 * pair + 1, top)

    top = score_range(even_ref, 0, 0, no_top)
    top = lax.fori_loop(0, blocks // 2 - 1, two_blocks, top)
    top = one_block(even_ref, odd_ref, blocks - 2, top)
    top = jnp.max(top, axis=0, keepdims=True)
    final = blocks - 1
    total = lax.fori_loop(
        0, bound_ref[1, final], functools.partial(weigh, odd_ref, top), no_total
    )
    finish(final, total)
    out_ref[...] = jnp.dot(
        unpick_ref[...], sorted_ref[...], preferred_element_type=jnp.float32
    ).astype(jnp.bfloat16)


def attend(bounds, query, kv, last, unpick):
    vmem = pl.BlockSpec(memory_space=pltpu.VMEM)
    count = unpick.shape[0]
    keys = kv.shape[0]
    return pl.pallas_call(
        attend_kernel,
        in_specs=[pl.BlockSpec(memory_space=pltpu.SMEM)] + [vmem] * 4,
        out_specs=vmem,
        out_shape=jax.ShapeDtypeStruct((count, GROUP * WIDTH), jnp.bfloat16),
        scratch_shapes=[
            pltpu.VMEM((WIDTH + 16, keys), jnp.bfloat16),
            pltpu.VMEM((keys, query.shape[1]), jnp.float32),
            pltpu.VMEM((keys, query.shape[1]), jnp.float32),
            pltpu.VMEM((count, GROUP * WIDTH), jnp.bfloat16),
        ],
        name="attend",
        compiler_params=pltpu.CompilerParams(vmem_limit_bytes=18 << 20),
    )(bounds, query, kv, last, unpick)


def mirrored_groups():
    sizes = [lax.axis_size(axis) for axis in ("yh", "z", "yl")]
    return [
        [
            (high * sizes[1] + z) * sizes[2] + (low if high == 0 else sizes[2] - 1 - low)
            for high in range(sizes[0])
            for z in range(sizes[1])
        ]
        for low in range(sizes[2])
    ]


def spread(x):
    groups = mirrored_groups()
    copies = jnp.broadcast_to(x[None], (len(groups[0]),) + x.shape)
    whole = lax.all_to_all(
        copies, ("yh", "z", "yl"), 0, 0, axis_index_groups=groups, tiled=True
    )
    return whole.reshape((-1,) + x.shape[1:])


def halves_kernel(whole_ref, low_ref, high_ref):
    half = low_ref.shape[0]
    low_ref[...] = whole_ref[:half]
    high_ref[...] = whole_ref[half:]


def halves(whole):
    vmem = pl.BlockSpec(memory_space=pltpu.VMEM)
    shape = jax.ShapeDtypeStruct((whole.shape[0] // 2, whole.shape[1]), whole.dtype)
    return pl.pallas_call(
        halves_kernel,
        in_specs=[vmem],
        out_specs=[vmem, vmem],
        out_shape=[shape, shape],
        name="halves",
        compiler_params=pltpu.CompilerParams(vmem_limit_bytes=6 << 20),
    )(whole)


def gather_weight(blocks):
    block_rows = blocks.shape[0]
    core = lax.axis_index("co")
    split = blocks.reshape(block_rows, KV_HEADS // 2, 2, LANES)
    mine = lax.dynamic_index_in_dim(split, core, 2, False).reshape(block_rows, -1)
    mine = jnp.pad(mine, ((0, PAD_ROWS - block_rows), (0, 0)))
    plane = spread(mine)
    up, down = ring(4, 1), ring(4, -1)
    low, high = halves(plane)

    def send(piece, pairs):
        return lax.ppermute(piece, "x", pairs)

    below_low = send(low, up)
    above_high = send(high, down)
    below_high = send(high, up)
    above_low = send(low, down)
    across_low = send(below_low, up)
    across_high = send(above_high, down)
    return (
        (low, high),
        (below_low, below_high, above_low, above_high),
        (across_low, across_high),
    )


def slot_order(block_of):
    x = lax.axis_index("x")
    xs = jnp.stack([x + 3, x + 1, x, x + 2]) % 4
    stored = jnp.arange(16)[None, :] * 4 + xs[:, None]
    return block_of[stored.reshape(-1)]


def attention(hidden, blocks, block_of, queries, key_pos, query_pos):
    core = lax.axis_index("co")
    seq_index = lax.axis_index(SEQ)
    seq = lax.axis_size(SEQ)
    rows = hidden.shape[1]
    keys = rows * seq
    block_rows = blocks.shape[0]
    query_rows = queries.shape[1]
    start = key_pos[0, 0] - rows * seq_index

    slots = slot_order(block_of)
    inner = jnp.arange(PAD_ROWS)
    source = jnp.where(
        inner[None, :] < block_rows, slots[:, None] * block_rows + inner[None, :], -1
    ).reshape(1, -1)

    high = (query_pos[0] >> 8).astype(jnp.bfloat16)
    low = (query_pos[0] & 255).astype(jnp.bfloat16)
    extra = jnp.concatenate(
        [
            jnp.broadcast_to(high[:, None, None], (query_rows, KV_HEADS, WIDTH)),
            jnp.broadcast_to(low[:, None, None], (query_rows, KV_HEADS, WIDTH)),
        ],
        -1,
    )
    payload = jnp.concatenate([queries[0].reshape(query_rows, KV_HEADS, GROUP * WIDTH), extra], -1)
    payload = payload.transpose(1, 0, 2)
    payload = lax.all_to_all(payload, SEQ, 0, 0, tiled=True)

    sign = jnp.asarray(np.where(np.arange(LANES) % WIDTH < WIDTH // 2, -1.0, 1.0), jnp.float32)
    freq = lane_frequencies(LANES)
    is_key = jnp.arange(LANES) < WIDTH
    mine = key_pos[0]
    theirs = mine + jnp.where(core == 0, rows, -rows)
    chip_pos = jnp.where(
        core == 0, jnp.concatenate([mine, theirs]), jnp.concatenate([theirs, mine])
    )
    key_angle = chip_pos.astype(jnp.float32)[:, None] * jnp.where(is_key, freq, 0.0)[None, :]
    key_cosine = jnp.cos(key_angle)
    key_sine = jnp.sin(key_angle) * jnp.where(is_key, sign, 0.0)
    plane, middle, far = gather_weight(blocks)
    depth = hidden.shape[2]
    wide = pl.cdiv(depth, LANES) * LANES
    padded = jnp.pad(hidden[0], ((0, 0), (0, wide - depth)))
    window = jnp.minimum(slots * block_rows // LANES * LANES, wide - 2 * LANES)
    own = reorder(padded, source, window)
    other = lax.ppermute(own, "co", ring(2, 1))

    total_queries = query_rows * seq
    payload = payload.reshape(total_queries, -1)
    query = payload[:, : GROUP * WIDTH]
    positions = (
        payload[:, GROUP * WIDTH].astype(jnp.float32) * 256.0
        + payload[:, GROUP * WIDTH + WIDTH].astype(jnp.float32)
    ).astype(jnp.int32)
    order = jnp.arange(total_queries)
    before = (positions[None, :] < positions[:, None]) | (
        (positions[None, :] == positions[:, None]) & (order[None, :] < order[:, None])
    )
    rank = jnp.sum(before.astype(jnp.int32), axis=1)
    pick_mask = rank[None, :] == order[:, None]
    sorted_pos = jnp.sum(jnp.where(pick_mask, positions[None, :], 0), axis=1)
    pick = pick_mask.astype(jnp.bfloat16)
    unpick = (rank[:, None] == order[None, :]).astype(jnp.bfloat16)
    last = sorted_pos - start
    by_block = last.reshape(-1, QUERY_BLOCK)
    bounds = jnp.stack([(by_block[:, 0] + 1) // KEY_BLOCK, by_block[:, -1] // KEY_BLOCK + 1])
    last_rows = jnp.tile(by_block, (1, GROUP))[:, None, :]

    query_angle = sorted_pos.astype(jnp.float32)[:, None] * freq[None, :]
    prepared = prepare(query, pick, jnp.cos(query_angle), jnp.sin(query_angle) * sign)

    place = core.reshape(1)
    total = partial_product(place, own, other, plane)
    total = partial_product(place, own, other, middle, total)
    kv = project(place, own, other, far, total, key_cosine, key_sine)
    kv = lax.all_to_all(kv, "yl", 0, 0, tiled=True).reshape(keys, LANES)
    context = attend(bounds, prepared, kv, last_rows, unpick)
    context = context.reshape(seq, query_rows, GROUP * WIDTH)
    context = lax.all_to_all(context, SEQ, 0, 0, tiled=True)
    return context.transpose(1, 0, 2).reshape(1, query_rows, HEADS * WIDTH)


def solution(mesh):
    fine = Mesh(mesh.devices.reshape(2, 8, 4, 4, 2), ROLL + SEQ)
    return jax.shard_map(
        attention,
        mesh=fine,
        in_specs=(
            P(ROLL, SEQ, None),
            P(ROLL, None),
            P(),
            P(ROLL, SEQ, None),
            P(ROLL, SEQ),
            P(ROLL, SEQ),
        ),
        out_specs=P(ROLL, SEQ, None),
        check_vma=False,
    )
```

```python
import functools

import jax
import jax.numpy as jnp
import numpy as np
from jax import lax
from jax.experimental import pallas as pl
from jax.experimental.pallas import tpu as pltpu
from jax.sharding import Mesh, PartitionSpec as P


HEADS = 64
KV_HEADS = 8
WIDTH = 64
GROUP = HEADS // KV_HEADS
LANES = 2 * WIDTH
ROPE_BASE = 150000.0
LOG2_E = 1.4426950408889634
PAD_ROWS = 48
QUERY_BLOCK = 32
KEY_BLOCK = 1024
ROLL = ("yh", "z", "x")
SEQ = ("yl", "co")


def lane_frequencies(lanes):
    half = WIDTH // 2
    freq = ROPE_BASE ** (-(jnp.arange(half).astype(jnp.float32) * 2.0 / WIDTH))
    return jnp.tile(freq, lanes // half)


def ring(size, step):
    return [(i, (i + step) % size) for i in range(size)]


def reorder_kernel(window_ref, source_ref, hidden_ref, out_ref):
    group = pl.program_id(0)
    index = lax.broadcasted_iota(jnp.int32, (2 * LANES, LANES), 0)
    lane = lax.broadcasted_iota(jnp.int32, (1, LANES), 1)
    slots = out_ref.shape[1] // PAD_ROWS
    for tile in range(out_ref.shape[1] // LANES):
        begin = tile * LANES
        source = source_ref[:, begin : begin + LANES]
        rows, picks = [], []
        for slot in range(slots):
            low, high = slot * PAD_ROWS - begin, (slot + 1) * PAD_ROWS - begin
            if high <= 0 or low >= LANES:
                continue
            window = pl.multiple_of(window_ref[group * slots + slot], LANES)
            place = jnp.where((lane >= low) & (lane < high), source - window, -1)
            picks.append(jnp.where(index == place, 1.0, 0.0).astype(jnp.bfloat16))
            rows.append(hidden_ref[:, pl.ds(window, 2 * LANES)])
        out_ref[:, begin : begin + LANES] = jnp.dot(
            jnp.concatenate(rows, 1),
            jnp.concatenate(picks, 0),
            preferred_element_type=jnp.float32,
        ).astype(jnp.bfloat16)


def reorder(hidden, source, window):
    rows, depth = hidden.shape
    columns = source.shape[1]
    tile = 8 * PAD_ROWS
    return pl.pallas_call(
        reorder_kernel,
        grid=(columns // tile,),
        in_specs=[
            pl.BlockSpec(memory_space=pltpu.SMEM),
            pl.BlockSpec((1, tile), lambda i: (0, i)),
            pl.BlockSpec((rows, depth), lambda i: (0, 0)),
        ],
        out_specs=pl.BlockSpec((rows, tile), lambda i: (0, i)),
        out_shape=jax.ShapeDtypeStruct((rows, columns), jnp.bfloat16),
        name="reorder_hidden",
        compiler_params=pltpu.CompilerParams(vmem_limit_bytes=16 << 20),
    )(window, source, hidden)


def swap_halves(x, lane):
    half = WIDTH // 2
    return jnp.where(
        lane % WIDTH < half,
        pltpu.roll(x, LANES - half, 1),
        pltpu.roll(x, half, 1),
    )


def product(hidden_ref, pieces):
    weight = jnp.concatenate([piece[...] for piece in pieces], 0)
    return jnp.dot(hidden_ref[...], weight, preferred_element_type=jnp.float32)


def partial_kernel(core_ref, own_ref, other_ref, *rest):
    pieces, out_ref = rest[:-1], rest[-1]
    rows = own_ref.shape[0]
    core = core_ref[0]
    for hidden_ref, place in ((own_ref, core), (other_ref, 1 - core)):
        here = pl.ds(pl.multiple_of(place * rows, rows), rows)
        out_ref[here, :] = product(hidden_ref, pieces)


def partial_product(core, own, other, pieces):
    vmem = pl.BlockSpec(memory_space=pltpu.VMEM)
    rows = own.shape[0]
    part = pl.BlockSpec((rows, sum(p.shape[0] for p in pieces)), lambda i: (0, 0))
    return pl.pallas_call(
        partial_kernel,
        grid=(1,),
        in_specs=[pl.BlockSpec(memory_space=pltpu.SMEM)]
        + [part, part]
        + [vmem] * len(pieces),
        out_specs=vmem,
        out_shape=jax.ShapeDtypeStruct((2 * rows, pieces[0].shape[1]), jnp.float32),
        name="partial_product",
        compiler_params=pltpu.CompilerParams(vmem_limit_bytes=18 << 20),
    )(core, own, other, *pieces)


def project_kernel(core_ref, own_ref, other_ref, total_ref, cos_ref, sin_ref, *rest):
    pieces, out_ref = rest[:-1], rest[-1]
    rows = own_ref.shape[0]
    core = core_ref[0]
    lane = lax.broadcasted_iota(jnp.int32, (rows, LANES), 1)
    for hidden_ref, place in ((own_ref, core), (other_ref, 1 - core)):
        here = pl.ds(pl.multiple_of(place * rows, rows), rows)
        total = total_ref[here, :] + product(hidden_ref, pieces)
        cosine = cos_ref[here, :]
        sine = sin_ref[here, :]
        for head in range(out_ref.shape[0]):
            x = total[:, head * LANES : (head + 1) * LANES]
            out_ref[head, here, :] = (x * cosine + swap_halves(x, lane) * sine).astype(
                jnp.bfloat16
            )


def project(core, own, other, pieces, total, cosine, sine):
    rows = own.shape[0]
    heads = total.shape[1] // LANES
    vmem = pl.BlockSpec(memory_space=pltpu.VMEM)
    depth = sum(piece.shape[0] for piece in pieces)
    part = pl.BlockSpec((rows, depth), lambda i: (0, own.shape[1] // depth - 1))
    return pl.pallas_call(
        project_kernel,
        grid=(1,),
        in_specs=[pl.BlockSpec(memory_space=pltpu.SMEM), part, part]
        + [vmem] * (3 + len(pieces)),
        out_specs=vmem,
        out_shape=jax.ShapeDtypeStruct((heads, 2 * rows, LANES), jnp.bfloat16),
        name="project",
        compiler_params=pltpu.CompilerParams(vmem_limit_bytes=20 << 20),
    )(core, own, other, total, cosine, sine, *pieces)


def prepare_kernel(query_ref, pick_ref, cos_ref, sin_ref, out_ref):
    rows = query_ref.shape[0]
    lane = lax.broadcasted_iota(jnp.int32, (rows, LANES), 1)
    pick = pick_ref[...]
    for pair in range(GROUP // 2):
        x = jnp.dot(
            pick,
            query_ref[:, pair * LANES : (pair + 1) * LANES],
            preferred_element_type=jnp.float32,
        )
        x = x * cos_ref[...] + swap_halves(x, lane) * sin_ref[...]
        x = x.astype(jnp.bfloat16).astype(jnp.float32) * (1.0 / 8.0)
        first = jnp.where(lane < WIDTH, x, 0.0).astype(jnp.bfloat16)
        second = jnp.where(lane < WIDTH, pltpu.roll(x, WIDTH, 1), 0.0).astype(jnp.bfloat16)
        for block in range(rows // QUERY_BLOCK):
            here = slice(block * QUERY_BLOCK, (block + 1) * QUERY_BLOCK)
            for head, value in ((2 * pair, first), (2 * pair + 1, second)):
                out_ref[block, head * QUERY_BLOCK : (head + 1) * QUERY_BLOCK, :] = value[here]


def prepare(query, pick, cosine, sine):
    rows = query.shape[0]
    vmem = pl.BlockSpec(memory_space=pltpu.VMEM)
    return pl.pallas_call(
        prepare_kernel,
        in_specs=[vmem] * 4,
        out_specs=vmem,
        out_shape=jax.ShapeDtypeStruct(
            (rows // QUERY_BLOCK, GROUP * QUERY_BLOCK, LANES), jnp.bfloat16
        ),
        name="prepare_queries",
        compiler_params=pltpu.CompilerParams(vmem_limit_bytes=6 << 20),
    )(query, pick, cosine, sine)


def attend_kernel(
    bound_ref, query_ref, kv_ref, last_ref, unpick_ref, out_ref, value_ref, even_ref, odd_ref, sorted_ref
):
    blocks = query_ref.shape[0]
    rows = query_ref.shape[1]
    keys = kv_ref.shape[0]
    value_ref[WIDTH:, :] = jnp.ones((value_ref.shape[0] - WIDTH, keys), jnp.bfloat16)
    for step in range(keys // KEY_BLOCK):
        here = slice(step * KEY_BLOCK, (step + 1) * KEY_BLOCK)
        value_ref[:WIDTH, here] = kv_ref[here, :].T[WIDTH:]
    key_index = lax.broadcasted_iota(jnp.int32, (KEY_BLOCK, rows), 0)
    lane = lax.broadcasted_iota(jnp.int32, (QUERY_BLOCK, LANES), 1)
    no_top = jnp.full((8, rows), -1e30, jnp.float32)
    no_total = jnp.zeros((value_ref.shape[0], rows), jnp.float32)

    def score(score_ref, block, masked, index, top):
        base = pl.multiple_of(index * KEY_BLOCK, KEY_BLOCK)
        scores = lax.dot_general(
            kv_ref[pl.ds(base, KEY_BLOCK), :],
            query_ref[block],
            (((1,), (1,)), ((), ())),
            preferred_element_type=jnp.float32,
        )
        scores = scores * LOG2_E
        if masked:
            scores = jnp.where(key_index <= last_ref[block] - base, scores, -1e30)
        score_ref[pl.ds(base, KEY_BLOCK), :] = scores
        return jnp.maximum(top, jnp.max(scores.reshape(-1, 8, rows), axis=0))

    def weigh(score_ref, top, index, total):
        base = pl.multiple_of(index * KEY_BLOCK, KEY_BLOCK)
        expo = jnp.exp2(score_ref[pl.ds(base, KEY_BLOCK), :] - top)
        return total + jnp.dot(
            value_ref[:, pl.ds(base, KEY_BLOCK)],
            expo.astype(jnp.bfloat16),
            preferred_element_type=jnp.float32,
        )

    def score_range(score_ref, block, begin, top):
        full, count = bound_ref[0, block], bound_ref[1, block]
        middle = jnp.maximum(begin, full)
        top = lax.fori_loop(
            begin, middle, functools.partial(score, score_ref, block, False), top
        )
        return lax.fori_loop(
            middle, count, functools.partial(score, score_ref, block, True), top
        )

    def finish(block, total):
        result = total[:WIDTH] / total[WIDTH : WIDTH + 1]
        result = jnp.concatenate([result, result], 0).T
        place = pl.multiple_of(block * QUERY_BLOCK, QUERY_BLOCK)
        for pair in range(GROUP // 2):
            even = result[2 * pair * QUERY_BLOCK : (2 * pair + 1) * QUERY_BLOCK]
            odd = result[(2 * pair + 1) * QUERY_BLOCK : (2 * pair + 2) * QUERY_BLOCK]
            sorted_ref[pl.ds(place, QUERY_BLOCK), pair * LANES : (pair + 1) * LANES] = jnp.where(
                lane < WIDTH, even, odd
            ).astype(jnp.bfloat16)

    def one_block(here_ref, next_ref, block, top):
        top = jnp.max(top, axis=0, keepdims=True)
        count = bound_ref[1, block]
        middle = jnp.minimum(count, bound_ref[0, block + 1])

        def both(masked, index, state):
            next_top, total = state
            return (
                score(next_ref, block + 1, masked, index, next_top),
                weigh(here_ref, top, index, total),
            )

        state = lax.fori_loop(0, middle, functools.partial(both, False), (no_top, no_total))
        state = lax.fori_loop(middle, count, functools.partial(both, True), state)
        finish(block, state[1])
        return score_range(next_ref, block + 1, count, state[0])

    def two_blocks(pair, top):
        top = one_block(even_ref, odd_ref, 2 * pair, top)
        return one_block(odd_ref, even_ref, 2 * pair + 1, top)

    top = score_range(even_ref, 0, 0, no_top)
    top = lax.fori_loop(0, blocks // 2 - 1, two_blocks, top)
    top = one_block(even_ref, odd_ref, blocks - 2, top)
    top = jnp.max(top, axis=0, keepdims=True)
    final = blocks - 1
    total = lax.fori_loop(
        0, bound_ref[1, final], functools.partial(weigh, odd_ref, top), no_total
    )
    finish(final, total)
    out_ref[...] = jnp.dot(
        unpick_ref[...], sorted_ref[...], preferred_element_type=jnp.float32
    ).astype(jnp.bfloat16)


def attend(bounds, query, kv, last, unpick):
    vmem = pl.BlockSpec(memory_space=pltpu.VMEM)
    count = unpick.shape[0]
    keys = kv.shape[0]
    return pl.pallas_call(
        attend_kernel,
        in_specs=[pl.BlockSpec(memory_space=pltpu.SMEM)] + [vmem] * 4,
        out_specs=vmem,
        out_shape=jax.ShapeDtypeStruct((count, GROUP * WIDTH), jnp.bfloat16),
        scratch_shapes=[
            pltpu.VMEM((WIDTH + 16, keys), jnp.bfloat16),
            pltpu.VMEM((keys, query.shape[1]), jnp.float32),
            pltpu.VMEM((keys, query.shape[1]), jnp.float32),
            pltpu.VMEM((count, GROUP * WIDTH), jnp.bfloat16),
        ],
        name="attend",
        compiler_params=pltpu.CompilerParams(vmem_limit_bytes=18 << 20),
    )(bounds, query, kv, last, unpick)


def mirrored_groups():
    sizes = [lax.axis_size(axis) for axis in ("yh", "z", "yl")]
    return [
        [
            (high * sizes[1] + z) * sizes[2] + (low if high == 0 else sizes[2] - 1 - low)
            for high in range(sizes[0])
            for z in range(sizes[1])
        ]
        for low in range(sizes[2])
    ]


def spread(copies):
    whole = lax.all_to_all(
        copies,
        ("yh", "z", "yl"),
        0,
        0,
        axis_index_groups=mirrored_groups(),
        tiled=True,
    )
    return whole.reshape(-1, copies.shape[2])


def halves_kernel(whole_ref, low_ref, high_ref, low_sem, high_sem):
    half = low_ref.shape[0]
    low = pltpu.make_async_copy(whole_ref.at[pl.ds(0, half)], low_ref, low_sem)
    high = pltpu.make_async_copy(whole_ref.at[pl.ds(half, half)], high_ref, high_sem)
    low.start()
    high.start()
    low.wait()
    high.wait()


def halves(whole):
    vmem = pl.BlockSpec(memory_space=pltpu.VMEM)
    shape = jax.ShapeDtypeStruct((whole.shape[0] // 2, whole.shape[1]), whole.dtype)
    return pl.pallas_call(
        halves_kernel,
        in_specs=[pl.BlockSpec(memory_space=pl.ANY)],
        out_specs=[vmem, vmem],
        out_shape=[shape, shape],
        scratch_shapes=[pltpu.SemaphoreType.DMA, pltpu.SemaphoreType.DMA],
        name="halves",
        compiler_params=pltpu.CompilerParams(vmem_limit_bytes=4 << 20),
    )(whole)


def copies_kernel(core_ref, blocks_ref, out_ref, mine_ref):
    block_rows = blocks_ref.shape[0]
    mine_ref[...] = jnp.zeros_like(mine_ref)
    for head in range(KV_HEADS // 2):
        column = pl.multiple_of((2 * head + core_ref[0]) * LANES, LANES)
        mine_ref[:block_rows, head * LANES : (head + 1) * LANES] = blocks_ref[
            :, pl.ds(column, LANES)
        ]
    for place in range(out_ref.shape[0]):
        out_ref[place] = mine_ref[...]


def weight_copies(blocks, core, count):
    vmem = pl.BlockSpec(memory_space=pltpu.VMEM)
    width = blocks.shape[1] // 2
    return pl.pallas_call(
        copies_kernel,
        in_specs=[pl.BlockSpec(memory_space=pltpu.SMEM), vmem],
        out_specs=vmem,
        out_shape=jax.ShapeDtypeStruct((count, PAD_ROWS, width), blocks.dtype),
        scratch_shapes=[pltpu.VMEM((PAD_ROWS, width), blocks.dtype)],
        name="weight_copies",
        compiler_params=pltpu.CompilerParams(vmem_limit_bytes=6 << 20),
    )(core.reshape(1), blocks)


def gather_weight(blocks):
    count = lax.axis_size("yh") * lax.axis_size("z")
    copies = weight_copies(blocks, lax.axis_index("co"), count)
    plane = spread(copies)
    up, down = ring(4, 1), ring(4, -1)
    low, high = halves(plane)

    def send(piece, pairs):
        return lax.ppermute(piece, "x", pairs)

    below_low = send(low, up)
    above_high = send(high, down)
    below_high = send(high, up)
    above_low = send(low, down)
    across_low = send(below_low, up)
    across_high = send(above_high, down)
    return (
        (low, high),
        (below_low, below_high, above_low, above_high),
        (across_low, across_high),
    )


def slot_order(block_of):
    x = lax.axis_index("x")
    xs = jnp.stack([x + 3, x + 1, x, x + 2]) % 4
    stored = jnp.arange(16)[None, :] * 4 + xs[:, None]
    return block_of[stored.reshape(-1)]


def attention(hidden, blocks, block_of, queries, key_pos, query_pos):
    core = lax.axis_index("co")
    seq_index = lax.axis_index(SEQ)
    seq = lax.axis_size(SEQ)
    rows = hidden.shape[1]
    keys = rows * seq
    block_rows = blocks.shape[0]
    query_rows = queries.shape[1]
    start = key_pos[0, 0] - rows * seq_index

    slots = slot_order(block_of)
    inner = jnp.arange(PAD_ROWS)
    source = jnp.where(
        inner[None, :] < block_rows, slots[:, None] * block_rows + inner[None, :], -1
    ).reshape(1, -1)

    high = (query_pos[0] >> 8).astype(jnp.bfloat16)
    low = (query_pos[0] & 255).astype(jnp.bfloat16)
    extra = jnp.concatenate(
        [
            jnp.broadcast_to(high[:, None, None], (query_rows, KV_HEADS, WIDTH)),
            jnp.broadcast_to(low[:, None, None], (query_rows, KV_HEADS, WIDTH)),
        ],
        -1,
    )
    payload = jnp.concatenate([queries[0].reshape(query_rows, KV_HEADS, GROUP * WIDTH), extra], -1)
    payload = payload.transpose(1, 0, 2)
    payload = lax.all_to_all(payload, SEQ, 0, 0, tiled=True)

    sign = jnp.asarray(np.where(np.arange(LANES) % WIDTH < WIDTH // 2, -1.0, 1.0), jnp.float32)
    freq = lane_frequencies(LANES)
    is_key = jnp.arange(LANES) < WIDTH
    mine = key_pos[0]
    theirs = mine + jnp.where(core == 0, rows, -rows)
    chip_pos = jnp.where(
        core == 0, jnp.concatenate([mine, theirs]), jnp.concatenate([theirs, mine])
    )
    key_angle = chip_pos.astype(jnp.float32)[:, None] * jnp.where(is_key, freq, 0.0)[None, :]
    key_cosine = jnp.cos(key_angle)
    key_sine = jnp.sin(key_angle) * jnp.where(is_key, sign, 0.0)
    plane, middle, far = gather_weight(blocks)
    depth = hidden.shape[2]
    wide = pl.cdiv(depth, LANES) * LANES
    padded = jnp.pad(hidden[0], ((0, 0), (0, wide - depth)))
    window = jnp.minimum(slots * block_rows // LANES * LANES, wide - 2 * LANES)
    own = reorder(padded, source, window)
    other = lax.ppermute(own, "co", ring(2, 1))

    total_queries = query_rows * seq
    payload = payload.reshape(total_queries, -1)
    query = payload[:, : GROUP * WIDTH]
    positions = (
        payload[:, GROUP * WIDTH].astype(jnp.float32) * 256.0
        + payload[:, GROUP * WIDTH + WIDTH].astype(jnp.float32)
    ).astype(jnp.int32)
    order = jnp.arange(total_queries)
    before = (positions[None, :] < positions[:, None]) | (
        (positions[None, :] == positions[:, None]) & (order[None, :] < order[:, None])
    )
    rank = jnp.sum(before.astype(jnp.int32), axis=1)
    pick_mask = rank[None, :] == order[:, None]
    sorted_pos = jnp.sum(jnp.where(pick_mask, positions[None, :], 0), axis=1)
    pick = pick_mask.astype(jnp.bfloat16)
    unpick = (rank[:, None] == order[None, :]).astype(jnp.bfloat16)
    last = sorted_pos - start
    by_block = last.reshape(-1, QUERY_BLOCK)
    bounds = jnp.stack([(by_block[:, 0] + 1) // KEY_BLOCK, by_block[:, -1] // KEY_BLOCK + 1])
    last_rows = jnp.tile(by_block, (1, GROUP))[:, None, :]

    query_angle = sorted_pos.astype(jnp.float32)[:, None] * freq[None, :]
    prepared = prepare(query, pick, jnp.cos(query_angle), jnp.sin(query_angle) * sign)

    place = core.reshape(1)
    total = partial_product(place, own, other, middle + plane)
    kv = project(place, own, other, far, total, key_cosine, key_sine)
    kv = lax.all_to_all(kv, "yl", 0, 0, tiled=True).reshape(keys, LANES)
    context = attend(bounds, prepared, kv, last_rows, unpick)
    context = context.reshape(seq, query_rows, GROUP * WIDTH)
    context = lax.all_to_all(context, SEQ, 0, 0, tiled=True)
    return context.transpose(1, 0, 2).reshape(1, query_rows, HEADS * WIDTH)


def solution(mesh):
    fine = Mesh(mesh.devices.reshape(2, 8, 4, 4, 2), ROLL + SEQ)
    return jax.shard_map(
        attention,
        mesh=fine,
        in_specs=(
            P(ROLL, SEQ, None),
            P(ROLL, None),
            P(),
            P(ROLL, SEQ, None),
            P(ROLL, SEQ),
            P(ROLL, SEQ),
        ),
        out_specs=P(ROLL, SEQ, None),
        check_vma=False,
    )
```
